128 devices in a mesh: sec: 4 (over y_lo, core), brick: 32 (over z, y_hi, x).
Axes of the slice: x: 4, y: 4 (y_hi: 2, y_lo: 2; y = y_hi * 2 + y_lo), z: 4, core: 2. Of those that a mesh axis runs over, the one named last changes fastest.
Arguments:
- potentials: float32 [4, 1024, 32, 128], P('sec', 'brick'), may hold values from -0.3 to 1.2
- coefficient: float32 [4, 1024, 32, 128], P('sec', 'brick'), may hold values from 0.04 to 0.32
- recovery: float32 [1024, 32, 128], P('brick'), may hold values from 0 to 1
- excitable: int32 [1024, 32, 128], P('brick'), may hold values 0 or 1
- row_of: int32 [32], P('brick'), may hold values from 0 to 2
Outputs:
- updated: float32 [4, 1024, 32, 128], P('sec', 'brick')
The draws below stay inside these ranges and needn't reach their ends.
Inputs may be any that keep to these rules, and one draw needn't show every extreme that they name: row_of[p] is the torso layer on which heart brick p lies.
All inputs are finite; a program needn't handle non-finite values. No bound on the sum of `excitable` on one device may be relied on, other than what follows from the above.
Results may differ from the reference program's by a relative error of at most 0.0003.
Values sent between devices are 32-bit elements; how exact they have to be, the bound alone decides.
No kernel may reach another device: no remote copies, remote signals or barrier semaphores. Data moves between devices by JAX's collectives and lax.ppermute only.
A program may use at most 64 MiB of HBM per device.

```python
import math
import jax
import jax.numpy as jnp

CX = 32
CY = 32
CZ = 128
SUBSTEPS = 8
SWEEPS = 16
STEPS = 2
NX = 1024
N_SEC = 4
N_BRICK = 32


def with_ends(entries, own_key, low, high):
    index_at = [jax.random.randint(jax.random.fold_in(own_key, axis), (), 0, length) for axis, length in enumerate(entries.shape)]
    longest = entries.shape.index(max(entries.shape))
    next_to = index_at[:longest] + [(index_at[longest] + 1) % entries.shape[longest]] + index_at[longest + 1:]
    return entries.at[tuple(index_at)].set(low).at[tuple(next_to)].set(high)


def levels(stream_key, shape, pieces, smallest, largest):
    level = 1.0
    for dim, shards_of in pieces:
        steps = jax.random.uniform(jax.random.fold_in(jax.random.fold_in(stream_key, 6), dim), (shards_of,), jnp.float32, smallest / len(pieces), largest / len(pieces))
        level = level * jnp.repeat(jnp.exp(steps), shape[dim] // shards_of).reshape((-1,) + (1,) * (len(shape) - 1 - dim))
    return level


def setup_inputs(seed: int = 0) -> dict:
    key_of = jax.random.split(jax.random.key(seed), 6)
    potentials = jnp.clip(-0.3 + 1.5 * jax.random.uniform(key_of[0], (N_SEC, NX, CY, CZ), jnp.float32) ** levels(key_of[0], (N_SEC, NX, CY, CZ), ((0, 4), (1, 32)), -0.2, 0.2), -0.3, 1.2)
    coefficient = jnp.clip(jnp.exp(math.log(0.32) - 2.0794415 * jax.random.uniform(key_of[1], (N_SEC, NX, CY, CZ), jnp.float32) ** levels(key_of[1], (N_SEC, NX, CY, CZ), ((0, 4), (1, 32)), -0.2, 0.2)), 0.04, 0.32)
    recovery = jnp.clip(1.0 * jax.random.uniform(key_of[2], (NX, CY, CZ), jnp.float32) ** levels(key_of[2], (NX, CY, CZ), ((0, 32),), -0.2, 0.2), 0.0, 1.0)
    excitable = with_ends((jax.random.randint(key_of[3], (NX, CY, CZ), 0, 5) < 4).astype(jnp.int32), jax.random.fold_in(key_of[3], 1), 0, 1)
    row_of = with_ends(jax.random.randint(key_of[4], (N_BRICK,), 0, N_SEC - 1), jax.random.fold_in(key_of[4], 1), 0, (N_SEC - 1) - 1).astype(jnp.int32)
    return dict(potentials=potentials, coefficient=coefficient, recovery=recovery, excitable=excitable, row_of=row_of)


coupling_gain = 0.1
ionic_timestep = 0.05
ionic_gain = 8.0
recovery_rate = 0.1
recovery_decay = 0.5
spectrum_low = 0.04
spectrum_high = 12.32


def chebyshev_weights(count):
    center = 0.5 * (spectrum_high + spectrum_low)
    spread = 0.5 * (spectrum_high - spectrum_low)
    ratio = center / spread
    current = 1.0 / ratio
    keeps = []
    pushes = []
    for number in range(count):
        following = 1.0 / (2.0 * ratio - current)
        keeps.append(following * current)
        pushes.append(2.0 * following / spread)
        current = following
    return center, keeps, pushes


def ionic(voltage, recovery, threshold, active):
    for substep in range(SUBSTEPS):
        drive = ionic_gain * voltage * (voltage - threshold) * (1.0 - voltage) - recovery
        relax = recovery_rate * (voltage - recovery_decay * recovery)
        voltage = voltage + ionic_timestep * active * drive
        recovery = recovery + ionic_timestep * active * relax
    return voltage, recovery


def heart_laplace(voltage):
    padded = jnp.pad(voltage, 1, mode="edge")
    total = padded[2:, 1:-1, 1:-1] + padded[:-2, 1:-1, 1:-1]
    total = total + padded[1:-1, 2:, 1:-1] + padded[1:-1, :-2, 1:-1]
    total = total + padded[1:-1, 1:-1, 2:] + padded[1:-1, 1:-1, :-2]
    return total - 6.0 * voltage


def beside_all(field):
    padded = jnp.pad(field, 1)
    total = padded[2:, 1:-1, 1:-1] + padded[:-2, 1:-1, 1:-1]
    total = total + padded[1:-1, 2:, 1:-1] + padded[1:-1, :-2, 1:-1]
    total = total + padded[1:-1, 1:-1, 2:] + padded[1:-1, 1:-1, :-2]
    return total


def to_grid(layers):
    return jnp.transpose(layers, (1, 0, 2, 3)).reshape(NX, 3 * CY, CZ)


def from_grid(field):
    return jnp.transpose(field.reshape(NX, 3, CY, CZ), (1, 0, 2, 3))


def reference(potentials, coefficient, recovery, excitable, row_of):
    voltage = potentials[3]
    threshold = coefficient[3]
    potential = to_grid(potentials[:3])
    absorption = to_grid(coefficient[:3])
    active = excitable.astype(jnp.float32)
    layers = jnp.arange(3, dtype=jnp.int32)
    select = (row_of[:, None] == layers[None, :]).astype(jnp.float32)[:, None, :, None, None]
    center, keeps, pushes = chebyshev_weights(SWEEPS - 1)
    source = heart_laplace(voltage)
    for coupling_step in range(STEPS):
        neighbours = beside_all(potential)
        current = (neighbours - 6.0 * potential).reshape(N_BRICK, CX, 3, CY, CZ)
        heart_current = jnp.sum(current * select, axis=2).reshape(NX, CY, CZ)
        placed = (source.reshape(N_BRICK, CX, 1, CY, CZ) * select).reshape(NX, 3 * CY, CZ)
        voltage, recovery = ionic(voltage, recovery, threshold, active)
        fresh = heart_laplace(voltage)
        voltage = voltage + coupling_gain * (fresh + heart_current)
        residual = placed - ((6.0 + absorption) * potential - neighbours)
        direction = residual / center
        for number in range(SWEEPS - 1):
            potential = potential + direction
            residual = residual - ((6.0 + absorption) * direction - beside_all(direction))
            direction = keeps[number] * direction + pushes[number] * residual
        potential = potential + direction
        source = fresh
    return jnp.concatenate([from_grid(potential), voltage[None]], axis=0)
```

```python
import jax
import jax.numpy as jnp
from jax import lax
from jax.experimental import pallas as pl
from jax.experimental.pallas import tpu as pltpu
from jax.sharding import PartitionSpec as P

SUBSTEPS = 8
SWEEPS = 16

coupling_gain = 0.1
ionic_timestep = 0.05
ionic_gain = 8.0
recovery_rate = 0.1
recovery_decay = 0.5
spectrum_low = 0.04
spectrum_high = 12.32

SLAB = 8
ROWS = 96
HEART = 32
SLOTS = 40
OWN = 16
PAD = 8
AXES = ("sec", "brick")
V0_AT, V1_AT, D_AT, ROW_AT, MSG = 96, 128, 160, 256, 264
PHI_PAD = 112
V_PAD = 48


def chebyshev_weights(count):
    center = 0.5 * (spectrum_high + spectrum_low)
    spread = 0.5 * (spectrum_high - spectrum_low)
    ratio = center / spread
    current = 1.0 / ratio
    weights = [(0.0, 1.0 / center)]
    for number in range(count):
        following = 1.0 / (2.0 * ratio - current)
        weights.append((following * current, 2.0 * following / spread))
        current = following
    return weights


WEIGHTS = chebyshev_weights(SWEEPS - 1)


def ionic(voltage, recovery, threshold, active):
    for substep in range(SUBSTEPS):
        drive = ionic_gain * voltage * (voltage - threshold) * (1.0 - voltage) - recovery
        relax = recovery_rate * (voltage - recovery_decay * recovery)
        voltage = voltage + ionic_timestep * active * drive
        recovery = recovery + ionic_timestep * active * relax
    return voltage, recovery


def lanes(shape):
    return lax.broadcasted_iota(jnp.int32, shape, len(shape) - 1)


def side_sum_zero(value):
    lane = lanes(value.shape)
    before = jnp.where(lane == 0, 0.0, pltpu.roll(value, 1, 1))
    after = jnp.where(lane == 127, 0.0, pltpu.roll(value, 127, 1))
    return before + after


def side_sum_edge(value):
    lane = lanes(value.shape)
    before = jnp.where(lane == 0, value, pltpu.roll(value, 1, 1))
    after = jnp.where(lane == 127, value, pltpu.roll(value, 127, 1))
    return before + after


def heart_laplace(ref, x):
    here = ref[x, PAD : PAD + HEART]
    total = ref[x - 1, PAD : PAD + HEART] + ref[x + 1, PAD : PAD + HEART]
    total = total + ref[x, PAD - 1 : PAD - 1 + HEART] + ref[x, PAD + 1 : PAD + 1 + HEART]
    return total + side_sum_edge(here) - 6.0 * here


def put_heart(ref, x, value):
    ref[x, PAD : PAD + HEART] = value
    ref[x, PAD - 1 : PAD] = value[0:1]
    ref[x, PAD + HEART : PAD + HEART + 1] = value[HEART - 1 : HEART]


def torso_current(ref, x, row):
    at = PAD + HEART * row
    here = ref[x, at : at + HEART]
    total = ref[x - 1, at : at + HEART] + ref[x + 1, at : at + HEART]
    total = total + ref[x, at - 1 : at - 1 + HEART] + ref[x, at + 1 : at + 1 + HEART]
    return total + side_sum_zero(here) - 6.0 * here


def solve(scal, even, odd, absorb, source):
    low_end, high_end = scal[4], scal[5]
    for level, (keep, push) in enumerate(WEIGHTS, 1):
        src, dst = (even, odd) if level % 2 else (odd, even)
        shift = 6.0 - (1.0 + keep) / push

        def plane(x, carry, src=src, dst=dst, keep=keep, push=push, shift=shift, level=level):
            for start in range(0, ROWS, 48):
                at, to = PAD + start, PAD + start + 48
                here = src[x, at:to]
                total = src[x - 1, at:to] + src[x + 1, at:to]
                total = total + (src[x, at - 1 : to - 1] + src[x, at + 1 : to + 1])
                total = total + side_sum_zero(here)
                total = total + source[x, start : start + 48]
                total = total - (absorb[x, start : start + 48] + shift) * here
                if level == 1:
                    dst[x, at:to] = push * total
                else:
                    dst[x, at:to] = push * total - keep * dst[x, at:to]
            return carry

        lax.fori_loop(
            jnp.maximum(level, low_end), jnp.minimum(SLOTS - level, high_end), plane, 0
        )


def clear_edges(even, odd):
    zero = jnp.zeros((PAD, 128), jnp.float32)

    def edge(x, carry):
        for ref in (even, odd):
            ref[x, 0:PAD] = zero
            ref[x, PAD + ROWS : PHI_PAD] = zero
        return carry

    lax.fori_loop(0, SLOTS, edge, 0)
    none = jnp.zeros((PHI_PAD, 128), jnp.float32)
    odd[OWN - 1] = none
    odd[OWN + 2 * SLAB] = none


def slots():
    return ((0, OWN, 1), (1, OWN + 2 * SLAB - 1, -1), (2, OWN - 1, -1), (3, 0, 1), (4, OWN + 2 * SLAB, 1))


def gather_kernel(scal, pot, coef, rec, exc, got_1, got_2, got_3, msg, aux, deep):
    sec, chunk, flip = scal[0], scal[1], scal[2]
    strip = jnp.full((8, 128), scal[3].astype(jnp.float32))

    def plane(u, carry):
        x = jnp.where(flip == 1, SLAB - 1 - u, u)
        whole = SLAB * chunk + x
        for number, ref in enumerate((None, got_1, got_2, got_3)):
            at = pl.multiple_of((sec ^ number) * HEART, HEART)
            if number == 0:
                msg[u, pl.ds(at, HEART)] = pot[whole]
                deep[u, pl.ds(at, HEART)] = coef[whole]
            else:
                msg[u, pl.ds(at, HEART)] = ref[0, x]
                deep[u, pl.ds(at, HEART)] = ref[1, x]
        msg[u, D_AT : D_AT + ROWS] = deep[u, 0:ROWS]
        threshold = deep[u, ROWS : ROWS + HEART]
        active = exc[whole].astype(jnp.float32)
        voltage, recovery = ionic(msg[u, V0_AT : V0_AT + HEART], rec[whole], threshold, active)
        msg[u, V1_AT : V1_AT + HEART] = voltage
        msg[u, ROW_AT : ROW_AT + 8] = strip
        aux[0, u] = threshold
        aux[1, u] = recovery
        aux[2, u] = active
        return carry

    lax.fori_loop(0, SLAB, plane, 0)


def first_kernel(scal, own, on, near, far, on2, aux, msg, held, absorb, later, even, odd, source, volt, volt_1):
    refs = (own, on, near, far, on2)
    clear_edges(even, odd)
    for number, first, step in slots():
        ref = refs[number]

        def unpack(u, carry, ref=ref, first=first, step=step):
            x = first + step * u
            even[x, PAD : PAD + ROWS] = ref[u, 0:ROWS]
            absorb[x] = ref[u, D_AT : D_AT + ROWS]
            put_heart(volt, x, ref[u, V0_AT : V0_AT + HEART])
            put_heart(volt_1, x, ref[u, V1_AT : V1_AT + HEART])
            return carry

        lax.fori_loop(0, SLAB, unpack, 0)

    @pl.when(scal[4] == OWN)
    def _():
        for ref in (volt, volt_1):
            ref[OWN - 1] = ref[OWN]

    @pl.when(scal[5] == OWN + 2 * SLAB)
    def _():
        for ref in (volt, volt_1):
            ref[OWN + 2 * SLAB] = ref[OWN + 2 * SLAB - 1]

    row = scal[3].astype(jnp.float32)
    for low, high, mark in (
        (1, OWN, near[0, ROW_AT : ROW_AT + 1]),
        (OWN, OWN + 2 * SLAB, jnp.full((1, 128), row)),
        (OWN + 2 * SLAB, SLOTS - 1, on2[0, ROW_AT : ROW_AT + 1]),
    ):
        mark = jnp.broadcast_to(mark, (HEART, 128))

        def place(x, carry, mark=mark):
            for ref, out in ((volt, source), (volt_1, later)):
                gain = heart_laplace(ref, x)
                for layer in range(3):
                    out[x, layer * HEART : (layer + 1) * HEART] = jnp.where(
                        mark == layer, gain, 0.0
                    )
            return carry

        lax.fori_loop(low, high, place, 0)

    for layer in range(3):

        @pl.when(scal[3] == layer)
        def _():
            def heart(u, carry):
                x = OWN + u
                gain = heart_laplace(volt_1, x) + torso_current(even, x, layer)
                voltage = volt_1[x, PAD : PAD + HEART] + coupling_gain * gain
                voltage, _ = ionic(voltage, aux[1, u], aux[0, u], aux[2, u])
                held[u] = voltage
                return carry

            lax.fori_loop(0, SLAB, heart, 0)

    solve(scal, even, odd, absorb, source)
    for u in range(SLAB):
        msg[u] = even[OWN + u, PAD : PAD + ROWS]
    msg[SLAB, 0:HEART] = held[0]
    msg[SLAB, HEART : 2 * HEART] = held[SLAB - 1]
    msg[SLAB, 2 * HEART : ROWS] = jnp.zeros((HEART, 128), jnp.float32)


def second_kernel(scal, own, on, near, far, on2, held, absorb, source, out, even, odd, volt, joined):
    refs = (own, on, near, far, on2)
    clear_edges(even, odd)
    for number, first, step in slots():
        ref = refs[number]

        def unpack(u, carry, ref=ref, first=first, step=step):
            even[first + step * u, PAD : PAD + ROWS] = ref[u]
            return carry

        lax.fori_loop(0, SLAB, unpack, 0)

    def keep(u, carry):
        put_heart(volt, u + 1, held[u])
        return carry

    lax.fori_loop(0, SLAB, keep, 0)
    put_heart(volt, 0, near[SLAB, 0:HEART])
    put_heart(volt, SLAB + 1, on[SLAB, HEART : 2 * HEART])

    @pl.when(scal[4] == OWN)
    def _():
        volt[0] = volt[1]

    for layer in range(3):

        @pl.when(scal[3] == layer)
        def _():
            def heart(u, carry):
                gain = heart_laplace(volt, u + 1) + torso_current(even, OWN + u, layer)
                joined[u, ROWS : ROWS + HEART] = held[u] + coupling_gain * gain
                return carry

            lax.fori_loop(0, SLAB, heart, 0)

    solve(scal, even, odd, absorb, source)

    sec, flip = scal[0], scal[2]

    def plane(u, carry):
        joined[u, 0:ROWS] = even[OWN + u, PAD : PAD + ROWS]
        x = jnp.where(flip == 1, SLAB - 1 - u, u)
        for number in range(4):
            at = pl.multiple_of((sec ^ number) * HEART, HEART)
            out[number, x] = joined[u, pl.ds(at, HEART)]
        return carry

    lax.fori_loop(0, SLAB, plane, 0)


def spread_kernel(scal, own, got_1, got_2, got_3, out):
    for number, ref in enumerate((own, got_1, got_2, got_3)):
        at = scal[6 + number] * SLAB
        for u in range(SLAB):
            out[at + u] = ref[u]


def chain(sections, bricks):
    order = []
    for brick in range(bricks):
        forward = (brick + brick // 4) % 2 == 1
        for step in range(sections):
            sec = step if forward else sections - 1 - step
            order.append(sec * bricks + brick)
    return order


VMEM = pl.BlockSpec(memory_space=pltpu.VMEM)
SMEM = pl.BlockSpec(memory_space=pltpu.SMEM)


def call(kernel, args, outs, scratch, name, flops):
    arrays = [jax.ShapeDtypeStruct(shape, jnp.float32) for shape in outs]
    return pl.pallas_call(
        kernel,
        out_shape=arrays,
        in_specs=[SMEM] + [VMEM] * (len(args) - 1),
        out_specs=[VMEM] * len(outs),
        scratch_shapes=[pltpu.VMEM(shape, jnp.float32) for shape in scratch],
        cost_estimate=pl.CostEstimate(flops=flops, bytes_accessed=4000000, transcendentals=0),
        name=name,
    )(*args)


def body(potentials, coefficient, recovery, excitable, row_of):
    pot, coef = potentials[0], coefficient[0]
    sections, bricks = lax.axis_size("sec"), lax.axis_size("brick")
    order = chain(sections, bricks)
    count = len(order)
    last = count - 1
    partner = [(order[i], order[i ^ 1]) for i in range(count)]
    facing = []
    for i in range(1, last, 2):
        facing += [(order[i], order[i + 1]), (order[i + 1], order[i])]
    beyond = [(order[i], order[i + 2]) for i in range(0, count - 2, 2)]
    beyond += [(order[i], order[i - 2]) for i in range(3, count, 2)]

    def across(number):
        return [(sec, sec ^ number) for sec in range(sections)]

    sec = lax.axis_index("sec")
    brick = lax.axis_index("brick")
    forward = (brick + brick // 4) % 2 == 1

    def chunk_of(section):
        return jnp.where(forward, section, sections - 1 - section)

    chunk = chunk_of(sec)
    place = brick * sections + chunk
    no_facing = (place == 0) | (place == last)
    partner_end = (place == 1) | (place == last - 1)
    scal = jnp.stack(
        [
            sec,
            chunk,
            chunk % 2,
            row_of[0],
            jnp.where(no_facing, OWN, 0),
            jnp.where(partner_end, OWN + 2 * SLAB, SLOTS),
        ]
        + [chunk_of(sec ^ number) for number in range(4)]
    ).astype(jnp.int32)

    got = []
    for number in (1, 2, 3):
        start = SLAB * chunk_of(sec ^ number)
        piece = jnp.stack(
            [
                lax.dynamic_slice_in_dim(pot, start, SLAB, 0),
                lax.dynamic_slice_in_dim(coef, start, SLAB, 0),
            ]
        )
        got.append(lax.ppermute(piece, "sec", across(number)))

    msg, aux = call(
        gather_kernel,
        (scal, pot, coef, recovery, excitable, *got),
        [(SLAB, MSG, 128), (3, SLAB, HEART, 128)],
        [(SLAB, 128, 128)],
        "gather",
        4_000_000,
    )

    def halos(value):
        near = lax.ppermute(value, AXES, facing)
        far = lax.ppermute(value, AXES, beyond)
        on = lax.ppermute(value, AXES, partner)
        on2 = lax.ppermute(near, AXES, partner)
        return value, on, near, far, on2

    phi = (SLOTS, PHI_PAD, 128)
    wide = (SLOTS, ROWS, 128)
    volt = (SLOTS, V_PAD, 128)
    msg, held, absorb, later = call(
        first_kernel,
        (scal, *halos(msg), aux),
        [(SLAB + 1, ROWS, 128), (SLAB, HEART, 128), wide, wide],
        [phi, phi, wide, volt, volt],
        "first",
        80_000_000,
    )
    (out,) = call(
        second_kernel,
        (scal, *halos(msg), held, absorb, later),
        [(4, SLAB, HEART, 128)],
        [phi, phi, (SLAB + 2, V_PAD, 128), (SLAB, 128, 128)],
        "second",
        80_000_000,
    )
    back = [out[0]] + [lax.ppermute(out[number], "sec", across(number)) for number in (1, 2, 3)]
    (result,) = call(
        spread_kernel,
        (scal, *back),
        [(sections * SLAB, HEART, 128)],
        [],
        "spread",
        100_000,
    )
    return result[None]


def solution(mesh):
    in_specs = (
        P("sec", "brick", None, None),
        P("sec", "brick", None, None),
        P("brick", None, None),
        P("brick", None, None),
        P("brick"),
    )
    out_specs = P("sec", "brick", None, None)
    return jax.shard_map(body, mesh=mesh, in_specs=in_specs, out_specs=out_specs, check_vma=False)
```

```python
import jax
import jax.numpy as jnp
from jax import lax
from jax.experimental import pallas as pl
from jax.experimental.pallas import tpu as pltpu
from jax.sharding import PartitionSpec as P

SUBSTEPS = 8
SWEEPS = 16

coupling_gain = 0.1
ionic_timestep = 0.05
ionic_gain = 8.0
recovery_rate = 0.1
recovery_decay = 0.5
spectrum_low = 0.04
spectrum_high = 12.32

SLAB = 8
ROWS = 96
HEART = 32
SLOTS = 40
OWN = 16
OFF = 1
PAD = 8
PART = 16
PARTS = ROWS // PART
AXES = ("sec", "brick")
V0_AT, V1_AT, D_AT, ROW_AT, MSG = 96, 128, 160, 256, 264
PHI_PAD = 112
V_PAD = 48


def chebyshev_weights(count):
    center = 0.5 * (spectrum_high + spectrum_low)
    spread = 0.5 * (spectrum_high - spectrum_low)
    ratio = center / spread
    current = 1.0 / ratio
    weights = [(0.0, 1.0 / center)]
    for number in range(count):
        following = 1.0 / (2.0 * ratio - current)
        weights.append((following * current, 2.0 * following / spread))
        current = following
    return weights


WEIGHTS = chebyshev_weights(SWEEPS - 1)
SHIFT = 6.0 - 0.5 * (spectrum_high + spectrum_low)


def ionic(voltage, recovery, threshold, active):
    for substep in range(SUBSTEPS):
        drive = ionic_gain * voltage * (voltage - threshold) * (1.0 - voltage) - recovery
        relax = recovery_rate * (voltage - recovery_decay * recovery)
        voltage = voltage + ionic_timestep * active * drive
        recovery = recovery + ionic_timestep * active * relax
    return voltage, recovery


def lanes(shape):
    return lax.broadcasted_iota(jnp.int32, shape, len(shape) - 1)


def side_sum_zero(value):
    lane = lanes(value.shape)
    before = jnp.where(lane == 0, 0.0, pltpu.roll(value, 1, 1))
    after = jnp.where(lane == 127, 0.0, pltpu.roll(value, 127, 1))
    return before + after


def side_sum_edge(value):
    lane = lanes(value.shape)
    before = jnp.where(lane == 0, value, pltpu.roll(value, 1, 1))
    after = jnp.where(lane == 127, value, pltpu.roll(value, 127, 1))
    return before + after


def heart_laplace(ref, x):
    here = ref[x, PAD : PAD + HEART]
    total = ref[x - 1, PAD : PAD + HEART] + ref[x + 1, PAD : PAD + HEART]
    total = total + ref[x, PAD - 1 : PAD - 1 + HEART] + ref[x, PAD + 1 : PAD + 1 + HEART]
    return total + side_sum_edge(here) - 6.0 * here


def put_heart(ref, x, value):
    ref[x, PAD : PAD + HEART] = value
    ref[x, PAD - 1 : PAD] = value[0:1]
    ref[x, PAD + HEART : PAD + HEART + 1] = value[HEART - 1 : HEART]


def torso_current(ref, x, row):
    at = PAD + HEART * row
    here = ref[x, at : at + HEART]
    total = ref[x - 1, at : at + HEART] + ref[x + 1, at : at + HEART]
    total = total + ref[x, at - 1 : at - 1 + HEART] + ref[x, at + 1 : at + 1 + HEART]
    return total + side_sum_zero(here) - 6.0 * here


def halves(value):
    high = value.astype(jnp.bfloat16)
    return high, (value - high.astype(jnp.float32)).astype(jnp.bfloat16)


def solve(scal, even, odd, absorb, source):
    accs = [pltpu.ACC(part % 2)((PART, 256), jnp.float32) for part in range(2 * PARTS)]
    pl.run_scoped(lambda *refs: sweeps(scal, even, odd, absorb, source, refs), *accs)


def sweeps(scal, even, odd, absorb, source, accs):
    accs = (accs[:PARTS], accs[PARTS:])
    row = lax.broadcasted_iota(jnp.int32, (256, 256), 0)
    column = lax.broadcasted_iota(jnp.int32, (256, 256), 1)
    same = (row >= 128) == (column >= 128)
    apart = jnp.abs(row - column)
    beside = ((same & (apart == 1)) | (apart == 128)).astype(jnp.bfloat16)
    none = jnp.zeros((PART, 256), jnp.bfloat16)
    for unit in range(2):
        pltpu.matmul_push_rhs(beside, 0, unit)
    for number, acc in enumerate(accs[0] + accs[1]):
        pltpu.matmul_acc_lhs(acc, none, load_staged_rhs=0 if number < 2 else None)
    for acc in accs[0] + accs[1]:
        pltpu.matmul_pop(acc)

    for level, (keep, push) in enumerate(WEIGHTS, 1):
        src, dst = (even, odd) if level % 2 else (odd, even)
        low = jnp.maximum(level, scal[4])
        high = jnp.minimum(SLOTS - level, scal[5])
        low = jnp.where(scal[5] < SLOTS, low - low % 2, low)
        pairs = (high - low + 1) // 2
        last = low + 2 * (pairs - 1)

        def begin(x, acc, src=src):
            for part in range(PARTS):
                at, to = PAD + PART * part, PAD + PART * (part + 1)
                high_0, low_0 = halves(src[x + OFF, at:to])
                high_1, low_1 = halves(src[x + OFF + 1, at:to])
                pltpu.matmul_acc_lhs(acc[part], jnp.concatenate([high_0, high_1], 1))
                pltpu.matmul_acc_lhs(acc[part], jnp.concatenate([low_0, low_1], 1))

        def finish(x, acc, src=src, dst=dst, level=level, keep=keep, push=push):
            for part in range(PARTS):
                start, stop = PART * part, PART * (part + 1)
                at, to = PAD + start, PAD + stop
                sums = pltpu.matmul_pop(acc[part])
                for plane in range(2):
                    here = x + plane
                    total = src[here + OFF - 1 + 2 * plane, at:to]
                    total = total + (src[here + OFF, at - 1 : to - 1] + src[here + OFF, at + 1 : to + 1])
                    total = total + source[here, start:stop]
                    total = total - absorb[here, start:stop] * src[here + OFF, at:to]
                    total = total + sums[:, 128 * plane : 128 * (plane + 1)]
                    if level == 1:
                        dst[here + OFF, at:to] = push * total
                    else:
                        dst[here + OFF, at:to] = push * total - keep * dst[here + OFF, at:to]

        begin(low, accs[0])

        def two_pairs(step, carry, low=low, last=last, begin=begin, finish=finish):
            x = low + 4 * step
            after = jnp.minimum(x + 2, last)
            begin(after, accs[1])
            finish(x, accs[0])
            begin(jnp.minimum(x + 4, last), accs[0])
            finish(after, accs[1])
            return carry

        lax.fori_loop(0, pairs // 2, two_pairs, 0)

        @pl.when(pairs % 2 == 1)
        def _(last=last, finish=finish):
            finish(last, accs[0])

        @pl.when(pairs % 2 == 0)
        def _():
            for acc in accs[0]:
                pltpu.matmul_pop(acc)


def clear_edges(even, odd):
    zero = jnp.zeros((PAD, 128), jnp.float32)

    def edge(x, carry):
        for ref in (even, odd):
            ref[x, 0:PAD] = zero
            ref[x, PAD + ROWS : PHI_PAD] = zero
        return carry

    lax.fori_loop(0, SLOTS + 2, edge, 0)
    none = jnp.zeros((PHI_PAD, 128), jnp.float32)
    odd[OFF + OWN - 1] = none
    odd[OFF + OWN + 2 * SLAB] = none


def slots():
    return ((0, OWN, 1), (1, OWN + 2 * SLAB - 1, -1), (2, OWN - 1, -1), (3, 0, 1), (4, OWN + 2 * SLAB, 1))


def gather_kernel(scal, pot, coef, rec, exc, got_1, got_2, got_3, msg, aux, deep):
    sec, chunk, flip = scal[0], scal[1], scal[2]
    strip = jnp.full((8, 128), scal[3].astype(jnp.float32))

    def plane(u, carry):
        x = jnp.where(flip == 1, SLAB - 1 - u, u)
        whole = SLAB * chunk + x
        for number, ref in enumerate((None, got_1, got_2, got_3)):
            at = pl.multiple_of((sec ^ number) * HEART, HEART)
            if number == 0:
                msg[u, pl.ds(at, HEART)] = pot[whole]
                deep[u, pl.ds(at, HEART)] = coef[whole]
            else:
                msg[u, pl.ds(at, HEART)] = ref[0, x]
                deep[u, pl.ds(at, HEART)] = ref[1, x]
        msg[u, D_AT : D_AT + ROWS] = deep[u, 0:ROWS]
        threshold = deep[u, ROWS : ROWS + HEART]
        active = exc[whole].astype(jnp.float32)
        voltage, recovery = ionic(msg[u, V0_AT : V0_AT + HEART], rec[whole], threshold, active)
        msg[u, V1_AT : V1_AT + HEART] = voltage
        msg[u, ROW_AT : ROW_AT + 8] = strip
        aux[0, u] = threshold
        aux[1, u] = recovery
        aux[2, u] = active
        return carry

    lax.fori_loop(0, SLAB, plane, 0)


def first_kernel(scal, own, on, near, far, on2, aux, msg, held, absorb, later, even, odd, source, volt, volt_1):
    refs = (own, on, near, far, on2)
    clear_edges(even, odd)
    for number, first, step in slots():
        ref = refs[number]

        def unpack(u, carry, ref=ref, first=first, step=step):
            x = first + step * u
            even[x + OFF, PAD : PAD + ROWS] = ref[u, 0:ROWS]
            absorb[x] = ref[u, D_AT : D_AT + ROWS] + SHIFT
            put_heart(volt, x, ref[u, V0_AT : V0_AT + HEART])
            put_heart(volt_1, x, ref[u, V1_AT : V1_AT + HEART])
            return carry

        lax.fori_loop(0, SLAB, unpack, 0)

    @pl.when(scal[4] == OWN)
    def _():
        for ref in (volt, volt_1):
            ref[OWN - 1] = ref[OWN]

    @pl.when(scal[5] == OWN + 2 * SLAB)
    def _():
        for ref in (volt, volt_1):
            ref[OWN + 2 * SLAB] = ref[OWN + 2 * SLAB - 1]

    row = scal[3].astype(jnp.float32)
    for low, high, mark in (
        (1, OWN, near[0, ROW_AT : ROW_AT + 1]),
        (OWN, OWN + 2 * SLAB, jnp.full((1, 128), row)),
        (OWN + 2 * SLAB, SLOTS - 1, on2[0, ROW_AT : ROW_AT + 1]),
    ):
        mark = jnp.broadcast_to(mark, (HEART, 128))

        def place(x, carry, mark=mark):
            for ref, out in ((volt, source), (volt_1, later)):
                gain = heart_laplace(ref, x)
                for layer in range(3):
                    out[x, layer * HEART : (layer + 1) * HEART] = jnp.where(
                        mark == layer, gain, 0.0
                    )
            return carry

        lax.fori_loop(low, high, place, 0)

    for layer in range(3):

        @pl.when(scal[3] == layer)
        def _():
            def heart(u, carry):
                x = OWN + u
                gain = heart_laplace(volt_1, x) + torso_current(even, x + OFF, layer)
                voltage = volt_1[x, PAD : PAD + HEART] + coupling_gain * gain
                voltage, _ = ionic(voltage, aux[1, u], aux[0, u], aux[2, u])
                held[u] = voltage
                return carry

            lax.fori_loop(0, SLAB, heart, 0)

    solve(scal, even, odd, absorb, source)
    for u in range(SLAB):
        msg[u] = even[OFF + OWN + u, PAD : PAD + ROWS]
    msg[SLAB, 0:HEART] = held[0]
    msg[SLAB, HEART : 2 * HEART] = held[SLAB - 1]
    msg[SLAB, 2 * HEART : ROWS] = jnp.zeros((HEART, 128), jnp.float32)


def second_kernel(scal, own, on, near, far, on2, held, absorb, source, *rest):
    outs, (even, odd, volt, joined) = rest[:4], rest[4:]
    refs = (own, on, near, far, on2)
    clear_edges(even, odd)
    for number, first, step in slots():
        ref = refs[number]

        def unpack(u, carry, ref=ref, first=first, step=step):
            even[OFF + first + step * u, PAD : PAD + ROWS] = ref[u]
            return carry

        lax.fori_loop(0, SLAB, unpack, 0)

    def keep(u, carry):
        put_heart(volt, u + 1, held[u])
        return carry

    lax.fori_loop(0, SLAB, keep, 0)
    put_heart(volt, 0, near[SLAB, 0:HEART])
    put_heart(volt, SLAB + 1, on[SLAB, HEART : 2 * HEART])

    @pl.when(scal[4] == OWN)
    def _():
        volt[0] = volt[1]

    for layer in range(3):

        @pl.when(scal[3] == layer)
        def _():
            def heart(u, carry):
                gain = heart_laplace(volt, u + 1) + torso_current(even, OWN + OFF + u, layer)
                joined[u, ROWS : ROWS + HEART] = held[u] + coupling_gain * gain
                return carry

            lax.fori_loop(0, SLAB, heart, 0)

    solve(scal, even, odd, absorb, source)

    sec, flip = scal[0], scal[2]

    def plane(u, carry):
        joined[u, 0:ROWS] = even[OFF + OWN + u, PAD : PAD + ROWS]
        x = jnp.where(flip == 1, SLAB - 1 - u, u)
        for number in range(4):
            at = pl.multiple_of((sec ^ number) * HEART, HEART)
            outs[number][x] = joined[u, pl.ds(at, HEART)]
        return carry

    lax.fori_loop(0, SLAB, plane, 0)


def spread_kernel(scal, own, got_1, got_2, got_3, out):
    for number, ref in enumerate((own, got_1, got_2, got_3)):
        at = scal[6 + number] * SLAB
        for u in range(SLAB):
            out[at + u] = ref[u]


def chain(sections, bricks):
    order = []
    for brick in range(bricks):
        forward = (brick + brick // 4) % 2 == 1
        for step in range(sections):
            sec = step if forward else sections - 1 - step
            order.append(sec * bricks + brick)
    return order


VMEM = pl.BlockSpec(memory_space=pltpu.VMEM)
SMEM = pl.BlockSpec(memory_space=pltpu.SMEM)


def call(kernel, args, outs, scratch, name, flops):
    arrays = [jax.ShapeDtypeStruct(shape, jnp.float32) for shape in outs]
    return pl.pallas_call(
        kernel,
        out_shape=arrays,
        in_specs=[SMEM] + [VMEM] * (len(args) - 1),
        out_specs=[VMEM] * len(outs),
        scratch_shapes=[pltpu.VMEM(shape, jnp.float32) for shape in scratch],
        cost_estimate=pl.CostEstimate(flops=flops, bytes_accessed=4000000, transcendentals=0),
        name=name,
    )(*args)


def body(potentials, coefficient, recovery, excitable, row_of):
    pot, coef = potentials[0], coefficient[0]
    sections, bricks = lax.axis_size("sec"), lax.axis_size("brick")
    order = chain(sections, bricks)
    count = len(order)
    last = count - 1
    partner = [(order[i], order[i ^ 1]) for i in range(count)]
    facing = []
    for i in range(1, last, 2):
        facing += [(order[i], order[i + 1]), (order[i + 1], order[i])]
    beyond = [(order[i], order[i + 2]) for i in range(0, count - 2, 2)]
    beyond += [(order[i], order[i - 2]) for i in range(3, count, 2)]

    def across(number):
        return [(sec, sec ^ number) for sec in range(sections)]

    sec = lax.axis_index("sec")
    brick = lax.axis_index("brick")
    forward = (brick + brick // 4) % 2 == 1

    def chunk_of(section):
        return jnp.where(forward, section, sections - 1 - section)

    chunk = chunk_of(sec)
    place = brick * sections + chunk
    no_facing = (place == 0) | (place == last)
    partner_end = (place == 1) | (place == last - 1)
    scal = jnp.stack(
        [
            sec,
            chunk,
            chunk % 2,
            row_of[0],
            jnp.where(no_facing, OWN, 0),
            jnp.where(partner_end, OWN + 2 * SLAB, SLOTS),
        ]
        + [chunk_of(sec ^ number) for number in range(4)]
    ).astype(jnp.int32)

    got = []
    for number in (1, 2, 3):
        start = SLAB * chunk_of(sec ^ number)
        piece = jnp.stack(
            [
                lax.dynamic_slice_in_dim(pot, start, SLAB, 0),
                lax.dynamic_slice_in_dim(coef, start, SLAB, 0),
            ]
        )
        got.append(lax.ppermute(piece, "sec", across(number)))

    msg, aux = call(
        gather_kernel,
        (scal, pot, coef, recovery, excitable, *got),
        [(SLAB, MSG, 128), (3, SLAB, HEART, 128)],
        [(SLAB, 128, 128)],
        "gather",
        4_000_000,
    )

    def halos(value):
        near = lax.ppermute(value, AXES, facing)
        far = lax.ppermute(value, AXES, beyond)
        on = lax.ppermute(value, AXES, partner)
        on2 = lax.ppermute(near, AXES, partner)
        return value, on, near, far, on2

    phi = (SLOTS + 2, PHI_PAD, 128)
    wide = (SLOTS, ROWS, 128)
    volt = (SLOTS, V_PAD, 128)
    msg, held, absorb, later = call(
        first_kernel,
        (scal, *halos(msg), aux),
        [(SLAB + 1, ROWS, 128), (SLAB, HEART, 128), wide, wide],
        [phi, phi, wide, volt, volt],
        "first",
        80_000_000,
    )
    outs = call(
        second_kernel,
        (scal, *halos(msg), held, absorb, later),
        [(SLAB, HEART, 128)] * 4,
        [phi, phi, (SLAB + 2, V_PAD, 128), (SLAB, 128, 128)],
        "second",
        80_000_000,
    )
    back = [outs[0]] + [lax.ppermute(outs[number], "sec", across(number)) for number in (1, 2, 3)]
    (result,) = call(
        spread_kernel,
        (scal, *back),
        [(sections * SLAB, HEART, 128)],
        [],
        "spread",
        100_000,
    )
    return result[None]


def solution(mesh):
    in_specs = (
        P("sec", "brick", None, None),
        P("sec", "brick", None, None),
        P("brick", None, None),
        P("brick", None, None),
        P("brick"),
    )
    out_specs = P("sec", "brick", None, None)
    return jax.shard_map(body, mesh=mesh, in_specs=in_specs, out_specs=out_specs, check_vma=False)
```

```python
import jax
import jax.numpy as jnp
from jax import lax
from jax.experimental import pallas as pl
from jax.experimental.pallas import tpu as pltpu
from jax.sharding import PartitionSpec as P

SUBSTEPS = 8
SWEEPS = 16

coupling_gain = 0.1
ionic_timestep = 0.05
ionic_gain = 8.0
recovery_rate = 0.1
recovery_decay = 0.5
spectrum_low = 0.04
spectrum_high = 12.32

SLAB = 8
ROWS = 96
HEART = 32
SLOTS = 40
OWN = 16
OFF = 1
PAD = 8
PART = 16
PARTS = ROWS // PART
AXES = ("sec", "brick")
V0_AT, V1_AT, D_AT, ROW_AT, MSG = 96, 128, 160, 256, 264
PHI_PAD = 112
V_PAD = 48


def chebyshev_weights(count):
    center = 0.5 * (spectrum_high + spectrum_low)
    spread = 0.5 * (spectrum_high - spectrum_low)
    ratio = center / spread
    current = 1.0 / ratio
    weights = [(0.0, 1.0 / center)]
    for number in range(count):
        following = 1.0 / (2.0 * ratio - current)
        weights.append((following * current, 2.0 * following / spread))
        current = following
    return weights


WEIGHTS = chebyshev_weights(SWEEPS - 1)
SHIFT = 6.0 - 0.5 * (spectrum_high + spectrum_low)


def ionic(voltage, recovery, threshold, active):
    for substep in range(SUBSTEPS):
        drive = ionic_gain * voltage * (voltage - threshold) * (1.0 - voltage) - recovery
        relax = recovery_rate * (voltage - recovery_decay * recovery)
        voltage = voltage + ionic_timestep * active * drive
        recovery = recovery + ionic_timestep * active * relax
    return voltage, recovery


def lanes(shape):
    return lax.broadcasted_iota(jnp.int32, shape, len(shape) - 1)


def side_sum_zero(value):
    lane = lanes(value.shape)
    before = jnp.where(lane == 0, 0.0, pltpu.roll(value, 1, 1))
    after = jnp.where(lane == 127, 0.0, pltpu.roll(value, 127, 1))
    return before + after


def side_sum_edge(value):
    lane = lanes(value.shape)
    before = jnp.where(lane == 0, value, pltpu.roll(value, 1, 1))
    after = jnp.where(lane == 127, value, pltpu.roll(value, 127, 1))
    return before + after


def heart_laplace(ref, x):
    here = ref[x, PAD : PAD + HEART]
    total = ref[x - 1, PAD : PAD + HEART] + ref[x + 1, PAD : PAD + HEART]
    total = total + ref[x, PAD - 1 : PAD - 1 + HEART] + ref[x, PAD + 1 : PAD + 1 + HEART]
    return total + side_sum_edge(here) - 6.0 * here


def put_heart(ref, x, value):
    ref[x, PAD : PAD + HEART] = value
    ref[x, PAD - 1 : PAD] = value[0:1]
    ref[x, PAD + HEART : PAD + HEART + 1] = value[HEART - 1 : HEART]


def torso_current(ref, x, row):
    at = PAD + HEART * row
    here = ref[x, at : at + HEART]
    total = ref[x - 1, at : at + HEART] + ref[x + 1, at : at + HEART]
    total = total + ref[x, at - 1 : at - 1 + HEART] + ref[x, at + 1 : at + 1 + HEART]
    return total + side_sum_zero(here) - 6.0 * here


def halves(value):
    high = value.astype(jnp.bfloat16)
    return high, (value - high.astype(jnp.float32)).astype(jnp.bfloat16)


def solve(scal, even, odd, absorb, source):
    accs = [pltpu.ACC(part % 2)((PART, 256), jnp.float32) for part in range(2 * PARTS)]
    pl.run_scoped(lambda *refs: sweeps(scal, even, odd, absorb, source, refs), *accs)


def sweeps(scal, even, odd, absorb, source, accs):
    accs = (accs[:PARTS], accs[PARTS:])
    row = lax.broadcasted_iota(jnp.int32, (256, 256), 0)
    column = lax.broadcasted_iota(jnp.int32, (256, 256), 1)
    same = (row >= 128) == (column >= 128)
    apart = jnp.abs(row - column)
    beside = ((same & (apart == 1)) | (apart == 128)).astype(jnp.bfloat16)
    none = jnp.zeros((PART, 256), jnp.bfloat16)
    for unit in range(2):
        pltpu.matmul_push_rhs(beside, 0, unit)
    for number, acc in enumerate(accs[0] + accs[1]):
        pltpu.matmul_acc_lhs(acc, none, load_staged_rhs=0 if number < 2 else None)
    for acc in accs[0] + accs[1]:
        pltpu.matmul_pop(acc)

    for level, (keep, push) in enumerate(WEIGHTS, 1):
        src, dst = (even, odd) if level % 2 else (odd, even)
        low = jnp.maximum(level, scal[4])
        high = jnp.minimum(SLOTS - level, scal[5])
        low = jnp.where(scal[5] < SLOTS, low - low % 2, low)
        pairs = (high - low + 1) // 2
        last = low + 2 * (pairs - 1)

        def begin(x, acc, src=src):
            for part in range(PARTS):
                at, to = PAD + PART * part, PAD + PART * (part + 1)
                high_0, low_0 = halves(src[x + OFF, at:to])
                high_1, low_1 = halves(src[x + OFF + 1, at:to])
                pltpu.matmul_acc_lhs(acc[part], jnp.concatenate([high_0, high_1], 1))
                pltpu.matmul_acc_lhs(acc[part], jnp.concatenate([low_0, low_1], 1))

        def finish(x, acc, src=src, dst=dst, level=level, keep=keep, push=push):
            for part in range(PARTS):
                start, stop = PART * part, PART * (part + 1)
                at, to = PAD + start, PAD + stop
                sums = pltpu.matmul_pop(acc[part])
                for plane in range(2):
                    here = x + plane
                    total = src[here + OFF - 1 + 2 * plane, at:to]
                    total = total + (src[here + OFF, at - 1 : to - 1] + src[here + OFF, at + 1 : to + 1])
                    total = total + source[here, start:stop]
                    total = total - absorb[here, start:stop] * src[here + OFF, at:to]
                    total = total + sums[:, 128 * plane : 128 * (plane + 1)]
                    if level == 1:
                        dst[here + OFF, at:to] = push * total
                    else:
                        dst[here + OFF, at:to] = push * total - keep * dst[here + OFF, at:to]

        begin(low, accs[0])

        def two_pairs(step, carry, low=low, last=last, begin=begin, finish=finish):
            x = low + 4 * step
            after = jnp.minimum(x + 2, last)
            begin(after, accs[1])
            finish(x, accs[0])
            begin(jnp.minimum(x + 4, last), accs[0])
            finish(after, accs[1])
            return carry

        lax.fori_loop(0, pairs // 2, two_pairs, 0)

        @pl.when(pairs % 2 == 1)
        def _(last=last, finish=finish):
            finish(last, accs[0])

        @pl.when(pairs % 2 == 0)
        def _():
            for acc in accs[0]:
                pltpu.matmul_pop(acc)


def clear_edges(even, odd):
    zero = jnp.zeros((PAD, 128), jnp.float32)

    def edge(x, carry):
        for ref in (even, odd):
            ref[x, 0:PAD] = zero
            ref[x, PAD + ROWS : PHI_PAD] = zero
        return carry

    lax.fori_loop(0, SLOTS + 2, edge, 0)
    none = jnp.zeros((PHI_PAD, 128), jnp.float32)
    odd[OFF + OWN - 1] = none
    odd[OFF + OWN + 2 * SLAB] = none


def slots():
    return ((0, OWN, 1), (1, OWN + 2 * SLAB - 1, -1), (2, OWN - 1, -1), (3, 0, 1), (4, OWN + 2 * SLAB, 1))


def gather_kernel(scal, pot, coef, rec, exc, got_1, got_2, got_3, msg, aux, deep):
    sec, chunk, flip = scal[0], scal[1], scal[2]
    strip = jnp.full((8, 128), scal[3].astype(jnp.float32))

    def plane(u, carry):
        x = jnp.where(flip == 1, SLAB - 1 - u, u)
        whole = SLAB * chunk + x
        for number, ref in enumerate((None, got_1, got_2, got_3)):
            at = pl.multiple_of((sec ^ number) * HEART, HEART)
            if number == 0:
                msg[u, pl.ds(at, HEART)] = pot[whole]
                deep[u, pl.ds(at, HEART)] = coef[whole]
            else:
                msg[u, pl.ds(at, HEART)] = ref[0, x]
                deep[u, pl.ds(at, HEART)] = ref[1, x]
        msg[u, D_AT : D_AT + ROWS] = deep[u, 0:ROWS]
        threshold = deep[u, ROWS : ROWS + HEART]
        active = exc[whole].astype(jnp.float32)
        voltage, recovery = ionic(msg[u, V0_AT : V0_AT + HEART], rec[whole], threshold, active)
        msg[u, V1_AT : V1_AT + HEART] = voltage
        msg[u, ROW_AT : ROW_AT + 8] = strip
        aux[0, u] = threshold
        aux[1, u] = recovery
        aux[2, u] = active
        return carry

    lax.fori_loop(0, SLAB, plane, 0)


def first_kernel(scal, own, on, near, far, on2, aux, msg, held, absorb, later, even, odd, source, volt, volt_1):
    refs = (own, on, near, far, on2)
    clear_edges(even, odd)
    for number, first, step in slots():
        ref = refs[number]

        def unpack(u, carry, ref=ref, first=first, step=step):
            x = first + step * u
            even[x + OFF, PAD : PAD + ROWS] = ref[u, 0:ROWS]
            absorb[x] = ref[u, D_AT : D_AT + ROWS] + SHIFT
            put_heart(volt, x, ref[u, V0_AT : V0_AT + HEART])
            put_heart(volt_1, x, ref[u, V1_AT : V1_AT + HEART])
            return carry

        lax.fori_loop(0, SLAB, unpack, 0)

    @pl.when(scal[4] == OWN)
    def _():
        for ref in (volt, volt_1):
            ref[OWN - 1] = ref[OWN]

    @pl.when(scal[5] == OWN + 2 * SLAB)
    def _():
        for ref in (volt, volt_1):
            ref[OWN + 2 * SLAB] = ref[OWN + 2 * SLAB - 1]

    row = scal[3].astype(jnp.float32)
    for low, high, mark in (
        (1, OWN, near[0, ROW_AT : ROW_AT + 1]),
        (OWN, OWN + 2 * SLAB, jnp.full((1, 128), row)),
        (OWN + 2 * SLAB, SLOTS - 1, on2[0, ROW_AT : ROW_AT + 1]),
    ):
        mark = jnp.broadcast_to(mark, (HEART, 128))

        def place(x, carry, mark=mark):
            for ref, out in ((volt, source), (volt_1, later)):
                gain = heart_laplace(ref, x)
                for layer in range(3):
                    out[x, layer * HEART : (layer + 1) * HEART] = jnp.where(
                        mark == layer, gain, 0.0
                    )
            return carry

        lax.fori_loop(low, high, place, 0)

    for layer in range(3):

        @pl.when(scal[3] == layer)
        def _():
            def heart(u, carry):
                x = OWN + u
                gain = heart_laplace(volt_1, x) + torso_current(even, x + OFF, layer)
                voltage = volt_1[x, PAD : PAD + HEART] + coupling_gain * gain
                voltage, _ = ionic(voltage, aux[1, u], aux[0, u], aux[2, u])
                held[u] = voltage
                return carry

            lax.fori_loop(0, SLAB, heart, 0)

    solve(scal, even, odd, absorb, source)
    for u in range(SLAB):
        msg[u] = even[OFF + OWN + u, PAD : PAD + ROWS]
    msg[SLAB, 0:HEART] = held[0]
    msg[SLAB, HEART : 2 * HEART] = held[SLAB - 1]
    msg[SLAB, 2 * HEART : ROWS] = jnp.zeros((HEART, 128), jnp.float32)


def second_kernel(scal, own, on, near, far, on2, held, absorb, source, *rest):
    outs, (even, odd, volt, joined) = rest[:4], rest[4:]
    refs = (own, on, near, far, on2)
    clear_edges(even, odd)
    for number, first, step in slots():
        ref = refs[number]

        def unpack(u, carry, ref=ref, first=first, step=step):
            even[OFF + first + step * u, PAD : PAD + ROWS] = ref[u]
            return carry

        lax.fori_loop(0, SLAB, unpack, 0)

    def keep(u, carry):
        put_heart(volt, u + 1, held[u])
        return carry

    lax.fori_loop(0, SLAB, keep, 0)
    put_heart(volt, 0, near[SLAB, 0:HEART])
    put_heart(volt, SLAB + 1, on[SLAB, HEART : 2 * HEART])

    @pl.when(scal[4] == OWN)
    def _():
        volt[0] = volt[1]

    for layer in range(3):

        @pl.when(scal[3] == layer)
        def _():
            def heart(u, carry):
                gain = heart_laplace(volt, u + 1) + torso_current(even, OWN + OFF + u, layer)
                joined[u, ROWS : ROWS + HEART] = held[u] + coupling_gain * gain
                return carry

            lax.fori_loop(0, SLAB, heart, 0)

    solve(scal, even, odd, absorb, source)

    sec, flip = scal[0], scal[2]

    def plane(u, carry):
        joined[u, 0:ROWS] = even[OFF + OWN + u, PAD : PAD + ROWS]
        x = jnp.where(flip == 1, SLAB - 1 - u, u)
        for number in range(4):
            at = pl.multiple_of((sec ^ number) * HEART, HEART)
            outs[number][x] = joined[u, pl.ds(at, HEART)]
        return carry

    lax.fori_loop(0, SLAB, plane, 0)


def spread_kernel(scal, own, got_1, got_2, got_3, out):
    for number, ref in enumerate((own, got_1, got_2, got_3)):
        at = scal[6 + number] * SLAB
        for u in range(SLAB):
            out[at + u] = ref[u]


def chain(sections, bricks):
    order = []
    for brick in range(bricks):
        forward = (brick + brick // 4) % 2 == 1
        for step in range(sections):
            sec = step if forward else sections - 1 - step
            order.append(sec * bricks + brick)
    return order


VMEM = pl.BlockSpec(memory_space=pltpu.VMEM)
SMEM = pl.BlockSpec(memory_space=pltpu.SMEM)


def call(kernel, args, outs, scratch, name, flops, limit=28):
    arrays = [jax.ShapeDtypeStruct(shape, jnp.float32) for shape in outs]
    return pl.pallas_call(
        kernel,
        out_shape=arrays,
        in_specs=[SMEM] + [VMEM] * (len(args) - 1),
        out_specs=[VMEM] * len(outs),
        scratch_shapes=[pltpu.VMEM(shape, jnp.float32) for shape in scratch],
        cost_estimate=pl.CostEstimate(flops=flops, bytes_accessed=4000000, transcendentals=0),
        compiler_params=pltpu.CompilerParams(vmem_limit_bytes=limit << 20),
        name=name,
    )(*args)


def body(potentials, coefficient, recovery, excitable, row_of):
    pot, coef = potentials[0], coefficient[0]
    sections, bricks = lax.axis_size("sec"), lax.axis_size("brick")
    order = chain(sections, bricks)
    count = len(order)
    last = count - 1
    partner = [(order[i], order[i ^ 1]) for i in range(count)]
    facing = []
    for i in range(1, last, 2):
        facing += [(order[i], order[i + 1]), (order[i + 1], order[i])]
    beyond = [(order[i], order[i + 2]) for i in range(0, count - 2, 2)]
    beyond += [(order[i], order[i - 2]) for i in range(3, count, 2)]

    def across(number):
        return [(sec, sec ^ number) for sec in range(sections)]

    sec = lax.axis_index("sec")
    brick = lax.axis_index("brick")
    forward = (brick + brick // 4) % 2 == 1

    def chunk_of(section):
        return jnp.where(forward, section, sections - 1 - section)

    chunk = chunk_of(sec)
    place = brick * sections + chunk
    no_facing = (place == 0) | (place == last)
    partner_end = (place == 1) | (place == last - 1)
    scal = jnp.stack(
        [
            sec,
            chunk,
            chunk % 2,
            row_of[0],
            jnp.where(no_facing, OWN, 0),
            jnp.where(partner_end, OWN + 2 * SLAB, SLOTS),
        ]
        + [chunk_of(sec ^ number) for number in range(4)]
    ).astype(jnp.int32)

    got = []
    for number in (1, 2, 3):
        start = SLAB * chunk_of(sec ^ number)
        piece = jnp.stack(
            [
                lax.dynamic_slice_in_dim(pot, start, SLAB, 0),
                lax.dynamic_slice_in_dim(coef, start, SLAB, 0),
            ]
        )
        got.append(lax.ppermute(piece, "sec", across(number)))

    msg, aux = call(
        gather_kernel,
        (scal, pot, coef, recovery, excitable, *got),
        [(SLAB, MSG, 128), (3, SLAB, HEART, 128)],
        [(SLAB, 128, 128)],
        "gather",
        4_000_000,
    )

    def halos(value):
        near = lax.ppermute(value, AXES, facing)
        far = lax.ppermute(value, AXES, beyond)
        on = lax.ppermute(value, AXES, partner)
        on2 = lax.ppermute(near, AXES, partner)
        return value, on, near, far, on2

    phi = (SLOTS + 2, PHI_PAD, 128)
    wide = (SLOTS, ROWS, 128)
    volt = (SLOTS, V_PAD, 128)
    msg, held, absorb, later = call(
        first_kernel,
        (scal, *halos(msg), aux),
        [(SLAB + 1, ROWS, 128), (SLAB, HEART, 128), wide, wide],
        [phi, phi, wide, volt, volt],
        "first",
        80_000_000,
    )
    outs = call(
        second_kernel,
        (scal, *halos(msg), held, absorb, later),
        [(SLAB, HEART, 128)] * 4,
        [phi, phi, (SLAB + 2, V_PAD, 128), (SLAB, 128, 128)],
        "second",
        80_000_000,
    )
    back = [outs[0]] + [lax.ppermute(outs[number], "sec", across(number)) for number in (1, 2, 3)]
    (result,) = call(
        spread_kernel,
        (scal, *back),
        [(sections * SLAB, HEART, 128)],
        [],
        "spread",
        100_000,
    )
    return result[None]


def solution(mesh):
    in_specs = (
        P("sec", "brick", None, None),
        P("sec", "brick", None, None),
        P("brick", None, None),
        P("brick", None, None),
        P("brick"),
    )
    out_specs = P("sec", "brick", None, None)
    return jax.shard_map(body, mesh=mesh, in_specs=in_specs, out_specs=out_specs, check_vma=False)
```

```python
import jax
import jax.numpy as jnp
from jax import lax
from jax.experimental import pallas as pl
from jax.experimental.pallas import tpu as pltpu
from jax.sharding import PartitionSpec as P

SUBSTEPS = 8
SWEEPS = 16

coupling_gain = 0.1
ionic_timestep = 0.05
ionic_gain = 8.0
recovery_rate = 0.1
recovery_decay = 0.5
spectrum_low = 0.04
spectrum_high = 12.32

SLAB = 8
ROWS = 96
HEART = 32
SLOTS = 40
OWN = 16
OFF = 1
PAD = 8
PART = 16
PARTS = ROWS // PART
AXES = ("sec", "brick")
V0_AT, V1_AT, D_AT, ROW_AT, MSG = 96, 128, 160, 256, 264
PHI_PAD = 112
V_PAD = 48


def chebyshev_weights(count):
    center = 0.5 * (spectrum_high + spectrum_low)
    spread = 0.5 * (spectrum_high - spectrum_low)
    ratio = center / spread
    current = 1.0 / ratio
    weights = [(0.0, 1.0 / center)]
    for _ in range(count):
        following = 1.0 / (2.0 * ratio - current)
        weights.append((following * current, 2.0 * following / spread))
        current = following
    return weights


WEIGHTS = chebyshev_weights(SWEEPS - 1)
SHIFT = 6.0 - 0.5 * (spectrum_high + spectrum_low)


def ionic(voltage, recovery, threshold, active):
    for _ in range(SUBSTEPS):
        drive = ionic_gain * voltage * (voltage - threshold) * (1.0 - voltage) - recovery
        relax = recovery_rate * (voltage - recovery_decay * recovery)
        voltage = voltage + ionic_timestep * active * drive
        recovery = recovery + ionic_timestep * active * relax
    return voltage, recovery


def lanes(shape):
    return lax.broadcasted_iota(jnp.int32, shape, len(shape) - 1)


def side_sum_zero(value):
    lane = lanes(value.shape)
    before = jnp.where(lane == 0, 0.0, pltpu.roll(value, 1, 1))
    after = jnp.where(lane == 127, 0.0, pltpu.roll(value, 127, 1))
    return before + after


def side_sum_edge(value):
    lane = lanes(value.shape)
    before = jnp.where(lane == 0, value, pltpu.roll(value, 1, 1))
    after = jnp.where(lane == 127, value, pltpu.roll(value, 127, 1))
    return before + after


def heart_laplace(ref, x):
    here = ref[x, PAD : PAD + HEART]
    total = ref[x - 1, PAD : PAD + HEART] + ref[x + 1, PAD : PAD + HEART]
    total = total + ref[x, PAD - 1 : PAD - 1 + HEART] + ref[x, PAD + 1 : PAD + 1 + HEART]
    return total + side_sum_edge(here) - 6.0 * here


def put_heart(ref, x, value):
    ref[x, PAD : PAD + HEART] = value
    ref[x, PAD - 1 : PAD] = value[0:1]
    ref[x, PAD + HEART : PAD + HEART + 1] = value[HEART - 1 : HEART]


def torso_current(ref, x, row):
    at = PAD + HEART * row
    here = ref[x, at : at + HEART]
    total = ref[x - 1, at : at + HEART] + ref[x + 1, at : at + HEART]
    total = total + ref[x, at - 1 : at - 1 + HEART] + ref[x, at + 1 : at + 1 + HEART]
    return total + side_sum_zero(here) - 6.0 * here


def halves(value):
    high = value.astype(jnp.bfloat16)
    return high, (value - high.astype(jnp.float32)).astype(jnp.bfloat16)


def sweep(scal, plan, even, odd, absorb, source):
    accs = [pltpu.ACC(part % 2)((PART, 256), jnp.float32) for part in range(2 * PARTS)]
    pl.run_scoped(lambda *refs: sweep_with(scal, plan, even, odd, absorb, source, refs), *accs)


def sweep_with(scal, plan, even, odd, absorb, source, accs):
    accs = (accs[:PARTS], accs[PARTS:])
    low_end, high_end = scal[4], scal[5]
    row = lax.broadcasted_iota(jnp.int32, (256, 256), 0)
    column = lax.broadcasted_iota(jnp.int32, (256, 256), 1)
    same = (row >= 128) == (column >= 128)
    apart = jnp.abs(row - column)
    beside = ((same & (apart == 1)) | (apart == 128)).astype(jnp.bfloat16)
    none = jnp.zeros((PART, 256), jnp.bfloat16)
    for unit in range(2):
        pltpu.matmul_push_rhs(beside, 0, unit)
    for number, acc in enumerate(accs[0] + accs[1]):
        pltpu.matmul_acc_lhs(acc, none, load_staged_rhs=0 if number < 2 else None)
    for acc in accs[0] + accs[1]:
        pltpu.matmul_pop(acc)

    def place(number, pair):
        _, runs = plan[number]
        first, size = runs[0]
        x = first + 2 * pair
        if len(runs) == 1:
            return x
        skip = runs[1][0] - first - size
        if isinstance(pair, int):
            return x + (skip if 2 * pair >= size else 0)
        return x + jnp.where(2 * pair >= size, skip, 0)

    def begin(number, pair, acc):
        level = plan[number][0]
        src = even if level % 2 else odd
        x = place(number, pair) + OFF
        for part in range(PARTS):
            at, to = PAD + PART * part, PAD + PART * (part + 1)
            high_0, low_0 = halves(src[x, at:to])
            high_1, low_1 = halves(src[x + 1, at:to])
            pltpu.matmul_acc_lhs(acc[part], jnp.concatenate([high_0, high_1], 1))
            pltpu.matmul_acc_lhs(acc[part], jnp.concatenate([low_0, low_1], 1))

    def finish(number, pair, acc):
        level = plan[number][0]
        src, dst = (even, odd) if level % 2 else (odd, even)
        x = place(number, pair)
        keeps, pushes = [], []
        for plane in range(2):
            inside = (x + plane >= low_end) & (x + plane < high_end)
            keeps.append(jnp.where(inside, WEIGHTS[level - 1][0], 0.0).astype(jnp.float32))
            pushes.append(jnp.where(inside, WEIGHTS[level - 1][1], 0.0).astype(jnp.float32))
        for part in range(PARTS):
            start, stop = PART * part, PART * (part + 1)
            at, to = PAD + start, PAD + stop
            sums = pltpu.matmul_pop(acc[part])
            for plane in range(2):
                here = x + plane
                total = src[here + OFF - 1 + 2 * plane, at:to]
                total = total + (src[here + OFF, at - 1 : to - 1] + src[here + OFF, at + 1 : to + 1])
                total = total + source[here, start:stop]
                total = total - absorb[here, start:stop] * src[here + OFF, at:to]
                total = pushes[plane] * (total + sums[:, 128 * plane : 128 * (plane + 1)])
                if level > 1:
                    total = total - keeps[plane] * dst[here + OFF, at:to]
                dst[here + OFF, at:to] = total

    one, other = accs
    begin(0, 0, one)
    for number, (_, runs) in enumerate(plan):
        pairs = sum(size for _, size in runs) // 2
        steps = (pairs - 1) // 2

        def two_pairs(step, carry, number=number, one=one, other=other):
            begin(number, 2 * step + 1, other)
            finish(number, 2 * step, one)
            begin(number, 2 * step + 2, one)
            finish(number, 2 * step + 1, other)
            return carry

        if steps:
            lax.fori_loop(0, steps, two_pairs, 0)
        pair = 2 * steps
        if pairs - pair == 2:
            begin(number, pair + 1, other)
            finish(number, pair, one)
            pair, one, other = pair + 1, other, one
        following = number + 1 < len(plan)
        if following and pairs > 2:
            begin(number + 1, 0, other)
        finish(number, pair, one)
        if following and pairs <= 2:
            begin(number + 1, 0, other)
        one, other = other, one


END = OWN + 2 * SLAB
INNER = [(k, [(OWN + k, 2 * SLAB - 2 * k)]) for k in range(1, SLAB)]
CLOSE = [(k, [(SLAB + k, SLAB), (END - k, SLAB)]) for k in range(1, SLAB + 1)]
OUTER = [(k, [(k, SLAB)]) for k in range(1, SLAB + 1)]
OUTER += [(k, [(k, SLOTS - 2 * k)]) for k in range(SLAB + 1, SWEEPS + 1)]


def clear_edges(even, odd):
    zero = jnp.zeros((PAD, 128), jnp.float32)

    def edge(x, carry):
        for ref in (even, odd):
            ref[x, 0:PAD] = zero
            ref[x, PAD + ROWS : PHI_PAD] = zero
        return carry

    lax.fori_loop(0, SLOTS + 2, edge, 0)


def gather_kernel(scal, pot, coef, rec, exc, got_1, got_2, got_3, msg, aux, deep):
    sec, chunk, flip = scal[0], scal[1], scal[2]
    strip = jnp.full((8, 128), scal[3].astype(jnp.float32))

    def plane(u, carry):
        x = jnp.where(flip == 1, SLAB - 1 - u, u)
        whole = SLAB * chunk + x
        for number, ref in enumerate((None, got_1, got_2, got_3)):
            at = pl.multiple_of((sec ^ number) * HEART, HEART)
            if number == 0:
                msg[u, pl.ds(at, HEART)] = pot[whole]
                deep[u, pl.ds(at, HEART)] = coef[whole]
            else:
                msg[u, pl.ds(at, HEART)] = ref[0, x]
                deep[u, pl.ds(at, HEART)] = ref[1, x]
        msg[u, D_AT : D_AT + ROWS] = deep[u, 0:ROWS]
        threshold = deep[u, ROWS : ROWS + HEART]
        active = exc[whole].astype(jnp.float32)
        voltage, recovery = ionic(msg[u, V0_AT : V0_AT + HEART], rec[whole], threshold, active)
        msg[u, V1_AT : V1_AT + HEART] = voltage
        msg[u, ROW_AT : ROW_AT + 8] = strip
        aux[0, u] = threshold
        aux[1, u] = recovery
        aux[2, u] = active
        return carry

    lax.fori_loop(0, SLAB, plane, 0)


def take(ref, first, step, even, absorb=None, volt=None, volt_1=None):
    def plane(u, carry):
        x = first + step * u
        even[x + OFF, PAD : PAD + ROWS] = ref[u, 0:ROWS]
        if absorb is not None:
            absorb[x] = ref[u, D_AT : D_AT + ROWS] + SHIFT
            put_heart(volt, x, ref[u, V0_AT : V0_AT + HEART])
            put_heart(volt_1, x, ref[u, V1_AT : V1_AT + HEART])
        return carry

    lax.fori_loop(0, SLAB, plane, 0)


def embed(low, high, mark, volt, volt_1, source, later):
    mark = jnp.broadcast_to(mark, (HEART, 128))

    def plane(x, carry):
        for ref, out in ((volt, source), (volt_1, later)):
            gain = heart_laplace(ref, x)
            for layer in range(3):
                out[x, layer * HEART : (layer + 1) * HEART] = jnp.where(mark == layer, gain, 0.0)
        return carry

    lax.fori_loop(low, high, plane, 0)


def on_layer(row, work):
    for layer in range(3):

        @pl.when(row == layer)
        def _():
            work(layer)


def couple(first, last, row, even, volt_1, aux, held):
    def work(layer):
        def plane(u, carry):
            x = OWN + u
            gain = heart_laplace(volt_1, x) + torso_current(even, x + OFF, layer)
            voltage = volt_1[x, PAD : PAD + HEART] + coupling_gain * gain
            held[u], _ = ionic(voltage, aux[1, u], aux[0, u], aux[2, u])
            return carry

        lax.fori_loop(first, last, plane, 0)

    on_layer(row, work)


def settle(first, last, row, even, volt, out):
    def work(layer):
        def plane(u, carry):
            gain = heart_laplace(volt, u + 1) + torso_current(even, OWN + OFF + u, layer)
            out[u] = volt[u + 1, PAD : PAD + HEART] + coupling_gain * gain
            return carry

        lax.fori_loop(first, last, plane, 0)

    on_layer(row, work)


def first_inner(scal, own, on, aux, even, odd, absorb, source, later, volt, volt_1, held, copy):
    def send(u, carry):
        copy[u] = own[u]
        return carry

    lax.fori_loop(0, SLAB, send, 0)
    clear_edges(even, odd)
    take(own, OWN, 1, even, absorb, volt, volt_1)
    take(on, END - 1, -1, even, absorb, volt, volt_1)
    row = jnp.full((1, 128), scal[3].astype(jnp.float32))
    embed(OWN + 1, END - 1, row, volt, volt_1, source, later)
    couple(1, SLAB, scal[3], even, volt_1, aux, held)
    sweep(scal, INNER, even, odd, absorb, source)


def first_close(scal, near, on2, aux, *refs):
    even, odd, absorb, source, later, volt, volt_1, held = refs[8:]
    take(near, OWN - 1, -1, even, absorb, volt, volt_1)
    take(on2, END, 1, even, absorb, volt, volt_1)

    @pl.when(scal[4] == OWN)
    def _():
        for ref in (volt, volt_1):
            ref[OWN - 1] = ref[OWN]

    @pl.when(scal[5] == END)
    def _():
        for ref in (volt, volt_1):
            ref[END] = ref[END - 1]

    row = jnp.full((1, 128), scal[3].astype(jnp.float32))
    for low, high, mark in (
        (SLAB + 1, OWN, near[0, ROW_AT : ROW_AT + 1]),
        (OWN, OWN + 1, row),
        (END - 1, END, row),
        (END, SLOTS - 1, on2[0, ROW_AT : ROW_AT + 1]),
    ):
        embed(low, high, mark, volt, volt_1, source, later)
    couple(0, 1, scal[3], even, volt_1, aux, held)
    sweep(scal, CLOSE, even, odd, absorb, source)


def first_outer(scal, far, held, *refs):
    msg, even, odd, absorb, source, later, volt, volt_1 = refs[7:]
    take(far, 0, 1, even, absorb, volt, volt_1)
    embed(1, SLAB + 1, far[0, ROW_AT : ROW_AT + 1], volt, volt_1, source, later)
    sweep(scal, OUTER, even, odd, absorb, source)
    for u in range(SLAB):
        msg[u] = even[OFF + OWN + u, PAD : PAD + ROWS]
    msg[SLAB, 0:HEART] = held[0]
    msg[SLAB, HEART : 2 * HEART] = held[SLAB - 1]
    msg[SLAB, 2 * HEART : ROWS] = jnp.zeros((HEART, 128), jnp.float32)


def second_inner(scal, own, on, held, absorb, source, even, odd, volt, out, copy):
    def keep(u, carry):
        copy[u] = own[u]
        put_heart(volt, u + 1, held[u])
        return carry

    lax.fori_loop(0, SLAB, keep, 0)
    clear_edges(even, odd)
    take(own, OWN, 1, even)
    take(on, END - 1, -1, even)
    put_heart(volt, SLAB + 1, on[SLAB, HEART : 2 * HEART])
    settle(1, SLAB, scal[3], even, volt, out)
    sweep(scal, INNER, even, odd, absorb, source)


def second_close(scal, near, on2, absorb, source, *refs):
    even, odd, volt, out = refs[4:]
    take(near, OWN - 1, -1, even)
    take(on2, END, 1, even)
    put_heart(volt, 0, near[SLAB, 0:HEART])

    @pl.when(scal[4] == OWN)
    def _():
        volt[0] = volt[1]

    settle(0, 1, scal[3], even, volt, out)
    sweep(scal, CLOSE, even, odd, absorb, source)


def second_outer(scal, far, absorb, source, voltage, *refs):
    outs, (even, odd), (joined,) = refs[2:6], refs[6:8], refs[8:]
    take(far, 0, 1, even)
    sweep(scal, OUTER, even, odd, absorb, source)
    sec, flip = scal[0], scal[2]

    def plane(u, carry):
        joined[u, 0:ROWS] = even[OFF + OWN + u, PAD : PAD + ROWS]
        joined[u, ROWS : ROWS + HEART] = voltage[u]
        x = jnp.where(flip == 1, SLAB - 1 - u, u)
        for number in range(4):
            at = pl.multiple_of((sec ^ number) * HEART, HEART)
            outs[number][x] = joined[u, pl.ds(at, HEART)]
        return carry

    lax.fori_loop(0, SLAB, plane, 0)


def spread_kernel(scal, own, got_1, got_2, got_3, out):
    for number, ref in enumerate((own, got_1, got_2, got_3)):
        at = scal[6 + number] * SLAB
        for u in range(SLAB):
            out[at + u] = ref[u]


def chain(sections, bricks):
    order = []
    for brick in range(bricks):
        forward = (brick + brick // 4) % 2 == 1
        for step in range(sections):
            sec = step if forward else sections - 1 - step
            order.append(sec * bricks + brick)
    return order


VMEM = pl.BlockSpec(memory_space=pltpu.VMEM)
SMEM = pl.BlockSpec(memory_space=pltpu.SMEM)


def call(kernel, args, outs, planes, scratch=(), state=(), limit=20):
    arrays = [jax.ShapeDtypeStruct(shape, jnp.float32) for shape in outs]
    arrays += [jax.ShapeDtypeStruct(ref.shape, ref.dtype) for ref in state]
    return pl.pallas_call(
        kernel,
        out_shape=arrays,
        in_specs=[SMEM] + [VMEM] * (len(args) + len(state) - 1),
        out_specs=[VMEM] * len(arrays),
        scratch_shapes=[pltpu.VMEM(shape, jnp.float32) for shape in scratch],
        input_output_aliases={len(args) + n: len(outs) + n for n in range(len(state))},
        compiler_params=pltpu.CompilerParams(vmem_limit_bytes=limit << 20),
        cost_estimate=pl.CostEstimate(
            flops=planes * 200_000, bytes_accessed=planes * 100_000, transcendentals=0
        ),
    )(*args, *state)


def body(potentials, coefficient, recovery, excitable, row_of):
    pot, coef = potentials[0], coefficient[0]
    sections, bricks = lax.axis_size("sec"), lax.axis_size("brick")
    order = chain(sections, bricks)
    count = len(order)
    last = count - 1
    partner = [(order[i], order[i ^ 1]) for i in range(count)]
    facing = []
    for i in range(1, last, 2):
        facing += [(order[i], order[i + 1]), (order[i + 1], order[i])]
    beyond = [(order[i], order[i + 2]) for i in range(0, count - 2, 2)]
    beyond += [(order[i], order[i - 2]) for i in range(3, count, 2)]

    def across(number):
        return [(sec, sec ^ number) for sec in range(sections)]

    sec = lax.axis_index("sec")
    brick = lax.axis_index("brick")
    forward = (brick + brick // 4) % 2 == 1

    def chunk_of(section):
        return jnp.where(forward, section, sections - 1 - section)

    chunk = chunk_of(sec)
    place = brick * sections + chunk
    no_facing = (place == 0) | (place == last)
    partner_end = (place == 1) | (place == last - 1)
    scal = jnp.stack(
        [
            sec,
            chunk,
            chunk % 2,
            row_of[0],
            jnp.where(no_facing, OWN, 0),
            jnp.where(partner_end, OWN + 2 * SLAB, SLOTS),
        ]
        + [chunk_of(sec ^ number) for number in range(4)]
    ).astype(jnp.int32)

    got = []
    for number in (1, 2, 3):
        start = SLAB * chunk_of(sec ^ number)
        piece = jnp.stack(
            [
                lax.dynamic_slice_in_dim(pot, start, SLAB, 0),
                lax.dynamic_slice_in_dim(coef, start, SLAB, 0),
            ]
        )
        got.append(lax.ppermute(piece, "sec", across(number)))

    msg, aux = call(
        gather_kernel,
        (scal, pot, coef, recovery, excitable, *got),
        [(SLAB, MSG, 128), (3, SLAB, HEART, 128)],
        20,
        scratch=[(SLAB, 128, 128)],
    )

    phi = (SLOTS + 2, PHI_PAD, 128)
    wide = (SLOTS, ROWS, 128)
    volt = (SLOTS, V_PAD, 128)
    heart = (SLAB, HEART, 128)

    def move(value, pairs):
        return lax.ppermute(value, AXES, pairs)

    near = move(msg, facing)
    on = move(msg, partner)
    *state, copy = call(
        first_inner,
        (scal, msg, on, aux),
        [phi, phi, wide, wide, wide, volt, volt, heart, msg.shape],
        56,
    )
    far = move(copy, beyond)
    on2 = move(near, partner)
    *state, held = call(first_close, (scal, near, on2, aux), [], 128, state=state)
    msg, _, _, absorb, _, later, _, _ = call(
        first_outer, (scal, far, held), [(SLAB + 1, ROWS, 128)], 184, state=state
    )

    near = move(msg, facing)
    on = move(msg, partner)
    *state, copy = call(
        second_inner,
        (scal, msg, on, held, absorb, later),
        [phi, phi, (SLAB + 2, V_PAD, 128), heart, (SLAB, ROWS, 128)],
        56,
    )
    far = move(copy, beyond)
    on2 = move(near, partner)
    even, odd, _, voltage = call(
        second_close, (scal, near, on2, absorb, later), [], 128, state=state
    )
    outs = call(
        second_outer,
        (scal, far, absorb, later, voltage),
        [heart] * 4,
        184,
        scratch=[(SLAB, 128, 128)],
        state=[even, odd],
    )[:4]
    back = [outs[0]] + [lax.ppermute(outs[number], "sec", across(number)) for number in (1, 2, 3)]
    (result,) = call(spread_kernel, (scal, *back), [(sections * SLAB, HEART, 128)], 5)
    return result[None]


def solution(mesh):
    in_specs = (
        P("sec", "brick", None, None),
        P("sec", "brick", None, None),
        P("brick", None, None),
        P("brick", None, None),
        P("brick"),
    )
    out_specs = P("sec", "brick", None, None)
    return jax.shard_map(body, mesh=mesh, in_specs=in_specs, out_specs=out_specs, check_vma=False)
```

```python
import jax
import jax.numpy as jnp
from jax import lax
from jax.experimental import pallas as pl
from jax.experimental.pallas import tpu as pltpu
from jax.sharding import PartitionSpec as P

SUBSTEPS = 8
SWEEPS = 16

coupling_gain = 0.1
ionic_timestep = 0.05
ionic_gain = 8.0
recovery_rate = 0.1
recovery_decay = 0.5
spectrum_low = 0.04
spectrum_high = 12.32

SLAB = 8
ROWS = 96
HEART = 32
SLOTS = 40
OWN = 16
OFF = 1
PAD = 8
PART = 16
PARTS = ROWS // PART
AXES = ("sec", "brick")
V0_AT, D_AT, V1_AT, ROW_AT, MSG = 96, 128, 224, 256, 264
FAR = V1_AT
PHI_PAD = 112
V_PAD = 48


def chebyshev_weights(count):
    center = 0.5 * (spectrum_high + spectrum_low)
    spread = 0.5 * (spectrum_high - spectrum_low)
    ratio = center / spread
    current = 1.0 / ratio
    weights = [(0.0, 1.0 / center)]
    for _ in range(count):
        following = 1.0 / (2.0 * ratio - current)
        weights.append((following * current, 2.0 * following / spread))
        current = following
    return weights


WEIGHTS = chebyshev_weights(SWEEPS - 1)
SHIFT = 6.0 - 0.5 * (spectrum_high + spectrum_low)


def ionic(voltage, recovery, threshold, active):
    for _ in range(SUBSTEPS):
        drive = ionic_gain * voltage * (voltage - threshold) * (1.0 - voltage) - recovery
        relax = recovery_rate * (voltage - recovery_decay * recovery)
        voltage = voltage + ionic_timestep * active * drive
        recovery = recovery + ionic_timestep * active * relax
    return voltage, recovery


def lanes(shape):
    return lax.broadcasted_iota(jnp.int32, shape, len(shape) - 1)


def side_sum_zero(value):
    lane = lanes(value.shape)
    before = jnp.where(lane == 0, 0.0, pltpu.roll(value, 1, 1))
    after = jnp.where(lane == 127, 0.0, pltpu.roll(value, 127, 1))
    return before + after


def side_sum_edge(value):
    lane = lanes(value.shape)
    before = jnp.where(lane == 0, value, pltpu.roll(value, 1, 1))
    after = jnp.where(lane == 127, value, pltpu.roll(value, 127, 1))
    return before + after


def heart_laplace(ref, x):
    here = ref[x, PAD : PAD + HEART]
    total = ref[x - 1, PAD : PAD + HEART] + ref[x + 1, PAD : PAD + HEART]
    total = total + ref[x, PAD - 1 : PAD - 1 + HEART] + ref[x, PAD + 1 : PAD + 1 + HEART]
    return total + side_sum_edge(here) - 6.0 * here


def put_heart(ref, x, value):
    ref[x, PAD : PAD + HEART] = value
    ref[x, PAD - 1 : PAD] = value[0:1]
    ref[x, PAD + HEART : PAD + HEART + 1] = value[HEART - 1 : HEART]


def torso_current(ref, x, row):
    at = PAD + HEART * row
    here = ref[x, at : at + HEART]
    total = ref[x - 1, at : at + HEART] + ref[x + 1, at : at + HEART]
    total = total + ref[x, at - 1 : at - 1 + HEART] + ref[x, at + 1 : at + 1 + HEART]
    return total + side_sum_zero(here) - 6.0 * here


def halves(value):
    high = value.astype(jnp.bfloat16)
    return high, (value - high.astype(jnp.float32)).astype(jnp.bfloat16)


def sweep(scal, plan, even, odd, absorb, source):
    accs = [pltpu.ACC(part % 2)((PART, 256), jnp.float32) for part in range(2 * PARTS)]
    pl.run_scoped(lambda *refs: sweep_with(scal, plan, even, odd, absorb, source, refs), *accs)


def sweep_with(scal, plan, even, odd, absorb, source, accs):
    accs = (accs[:PARTS], accs[PARTS:])
    low_end, high_end = scal[4], scal[5]
    row = lax.broadcasted_iota(jnp.int32, (256, 256), 0)
    column = lax.broadcasted_iota(jnp.int32, (256, 256), 1)
    same = (row >= 128) == (column >= 128)
    apart = jnp.abs(row - column)
    beside = ((same & (apart == 1)) | (apart == 128)).astype(jnp.bfloat16)
    none = jnp.zeros((PART, 256), jnp.bfloat16)
    for unit in range(2):
        pltpu.matmul_push_rhs(beside, 0, unit)
    for number, acc in enumerate(accs[0] + accs[1]):
        pltpu.matmul_acc_lhs(acc, none, load_staged_rhs=0 if number < 2 else None)
    for acc in accs[0] + accs[1]:
        pltpu.matmul_pop(acc)

    def place(number, pair):
        _, runs = plan[number]
        first, size = runs[0]
        x = first + 2 * pair
        if len(runs) == 1:
            return x
        skip = runs[1][0] - first - size
        if isinstance(pair, int):
            return x + (skip if 2 * pair >= size else 0)
        return x + jnp.where(2 * pair >= size, skip, 0)

    def begin(number, pair, acc):
        level = plan[number][0]
        src = even if level % 2 else odd
        x = place(number, pair) + OFF
        for part in range(PARTS):
            at, to = PAD + PART * part, PAD + PART * (part + 1)
            high_0, low_0 = halves(src[x, at:to])
            high_1, low_1 = halves(src[x + 1, at:to])
            pltpu.matmul_acc_lhs(acc[part], jnp.concatenate([high_0, high_1], 1))
            pltpu.matmul_acc_lhs(acc[part], jnp.concatenate([low_0, low_1], 1))

    def finish(number, pair, acc):
        level = plan[number][0]
        src, dst = (even, odd) if level % 2 else (odd, even)
        x = place(number, pair)
        keeps, pushes = [], []
        for plane in range(2):
            inside = (x + plane >= low_end) & (x + plane < high_end)
            keeps.append(jnp.where(inside, WEIGHTS[level - 1][0], 0.0).astype(jnp.float32))
            pushes.append(jnp.where(inside, WEIGHTS[level - 1][1], 0.0).astype(jnp.float32))
        for part in range(PARTS):
            start, stop = PART * part, PART * (part + 1)
            at, to = PAD + start, PAD + stop
            sums = pltpu.matmul_pop(acc[part])
            for plane in range(2):
                here = x + plane
                total = src[here + OFF - 1 + 2 * plane, at:to]
                total = total + (src[here + OFF, at - 1 : to - 1] + src[here + OFF, at + 1 : to + 1])
                total = total + source[here, start:stop]
                total = total - absorb[here, start:stop] * src[here + OFF, at:to]
                total = pushes[plane] * (total + sums[:, 128 * plane : 128 * (plane + 1)])
                if level > 1:
                    total = total - keeps[plane] * dst[here + OFF, at:to]
                dst[here + OFF, at:to] = total

    one, other = accs
    begin(0, 0, one)
    for number, (_, runs) in enumerate(plan):
        pairs = sum(size for _, size in runs) // 2
        steps = (pairs - 1) // 2

        def two_pairs(step, carry, number=number, one=one, other=other):
            begin(number, 2 * step + 1, other)
            finish(number, 2 * step, one)
            begin(number, 2 * step + 2, one)
            finish(number, 2 * step + 1, other)
            return carry

        if steps:
            lax.fori_loop(0, steps, two_pairs, 0)
        pair = 2 * steps
        if pairs - pair == 2:
            begin(number, pair + 1, other)
            finish(number, pair, one)
            pair, one, other = pair + 1, other, one
        following = number + 1 < len(plan)
        if following and pairs > 2:
            begin(number + 1, 0, other)
        finish(number, pair, one)
        if following and pairs <= 2:
            begin(number + 1, 0, other)
        one, other = other, one


END = OWN + 2 * SLAB
INNER = [(k, [(OWN + k, 2 * SLAB - 2 * k)]) for k in range(1, SLAB)]
LEFT = [(k, [(SLAB + k, SLAB)]) for k in range(1, SLAB + 1)]
RIGHT = [(k, [(END - k, SLAB)]) for k in range(1, SLAB + 1)]
OUTER = [(k, [(k, SLAB)]) for k in range(1, SLAB + 1)]
OUTER += [(k, [(k, SLOTS - 2 * k)]) for k in range(SLAB + 1, SWEEPS + 1)]


def clear_edges(even, odd):
    zero = jnp.zeros((PAD, 128), jnp.float32)

    def edge(x, carry):
        for ref in (even, odd):
            ref[x, 0:PAD] = zero
            ref[x, PAD + ROWS : PHI_PAD] = zero
        return carry

    lax.fori_loop(0, SLOTS + 2, edge, 0)


def gather_kernel(scal, pot, coef, rec, exc, got_1, got_2, got_3, msg, aux, deep):
    sec, chunk, flip = scal[0], scal[1], scal[2]
    strip = jnp.full((8, 128), scal[3].astype(jnp.float32))

    def plane(u, carry):
        x = jnp.where(flip == 1, SLAB - 1 - u, u)
        whole = SLAB * chunk + x
        for number, ref in enumerate((None, got_1, got_2, got_3)):
            at = pl.multiple_of((sec ^ number) * HEART, HEART)
            if number == 0:
                msg[u, pl.ds(at, HEART)] = pot[whole]
                deep[u, pl.ds(at, HEART)] = coef[whole]
            else:
                msg[u, pl.ds(at, HEART)] = ref[0, x]
                deep[u, pl.ds(at, HEART)] = ref[1, x]
        msg[u, D_AT : D_AT + ROWS] = deep[u, 0:ROWS]
        threshold = deep[u, ROWS : ROWS + HEART]
        active = exc[whole].astype(jnp.float32)
        voltage, recovery = ionic(msg[u, V0_AT : V0_AT + HEART], rec[whole], threshold, active)
        msg[u, V1_AT : V1_AT + HEART] = voltage
        msg[u, ROW_AT : ROW_AT + 8] = strip
        aux[0, u] = threshold
        aux[1, u] = recovery
        aux[2, u] = active
        return carry

    lax.fori_loop(0, SLAB, plane, 0)


def take(ref, first, step, even, absorb=None, volt=None, volt_1=None):
    def plane(u, carry):
        x = first + step * u
        even[x + OFF, PAD : PAD + ROWS] = ref[u, 0:ROWS]
        if absorb is not None:
            absorb[x] = ref[u, D_AT : D_AT + ROWS] + SHIFT
            put_heart(volt, x, ref[u, V0_AT : V0_AT + HEART])
        if volt_1 is not None:
            put_heart(volt_1, x, ref[u, V1_AT : V1_AT + HEART])
        return carry

    lax.fori_loop(0, SLAB, plane, 0)


def embed(low, high, mark, *fields):
    mark = jnp.broadcast_to(mark, (HEART, 128))

    def plane(x, carry):
        for ref, out in fields:
            gain = heart_laplace(ref, x)
            for layer in range(3):
                out[x, layer * HEART : (layer + 1) * HEART] = jnp.where(mark == layer, gain, 0.0)
        return carry

    lax.fori_loop(low, high, plane, 0)


def on_layer(row, work):
    for layer in range(3):

        @pl.when(row == layer)
        def _():
            work(layer)


def couple(first, last, row, even, volt_1, aux, held):
    def work(layer):
        def plane(u, carry):
            x = OWN + u
            gain = heart_laplace(volt_1, x) + torso_current(even, x + OFF, layer)
            voltage = volt_1[x, PAD : PAD + HEART] + coupling_gain * gain
            held[u], _ = ionic(voltage, aux[1, u], aux[0, u], aux[2, u])
            return carry

        lax.fori_loop(first, last, plane, 0)

    on_layer(row, work)


def settle(first, last, row, even, volt, out):
    def work(layer):
        def plane(u, carry):
            gain = heart_laplace(volt, u + 1) + torso_current(even, OWN + OFF + u, layer)
            out[u] = volt[u + 1, PAD : PAD + HEART] + coupling_gain * gain
            return carry

        lax.fori_loop(first, last, plane, 0)

    on_layer(row, work)


def first_inner(scal, own, on, aux, even, odd, absorb, source, later, volt, volt_1, held, copy):
    def send(u, carry):
        copy[u] = own[u, 0:FAR]
        return carry

    lax.fori_loop(0, SLAB, send, 0)
    clear_edges(even, odd)
    take(own, OWN, 1, even, absorb, volt, volt_1)
    take(on, END - 1, -1, even, absorb, volt, volt_1)
    row = jnp.full((1, 128), scal[3].astype(jnp.float32))
    embed(OWN + 1, END - 1, row, (volt, source), (volt_1, later))
    couple(1, SLAB, scal[3], even, volt_1, aux, held)
    sweep(scal, INNER, even, odd, absorb, source)


def first_left(scal, near, aux, *refs):
    even, odd, absorb, source, later, volt, volt_1, held = refs[8:]
    take(near, OWN - 1, -1, even, absorb, volt, volt_1)

    @pl.when(scal[4] == OWN)
    def _():
        for ref in (volt, volt_1):
            ref[OWN - 1] = ref[OWN]

    row = jnp.full((1, 128), scal[3].astype(jnp.float32))
    fields = ((volt, source), (volt_1, later))
    embed(SLAB + 1, OWN, near[0, ROW_AT : ROW_AT + 1], *fields)
    embed(OWN, OWN + 1, row, *fields)
    couple(0, 1, scal[3], even, volt_1, aux, held)
    sweep(scal, LEFT, even, odd, absorb, source)


def first_right(scal, on2, *refs):
    even, odd, absorb, source, later, volt, volt_1 = refs[7:]
    take(on2, END, 1, even, absorb, volt, volt_1)

    @pl.when(scal[5] == END)
    def _():
        for ref in (volt, volt_1):
            ref[END] = ref[END - 1]

    row = jnp.full((1, 128), scal[3].astype(jnp.float32))
    fields = ((volt, source), (volt_1, later))
    embed(END - 1, END, row, *fields)
    embed(END, SLOTS - 1, on2[0, ROW_AT : ROW_AT + 1], *fields)
    sweep(scal, RIGHT, even, odd, absorb, source)


def first_outer(scal, far, near, held, *refs):
    msg, even, odd, absorb, source, volt = refs[5:]
    take(far, 0, 1, even, absorb, volt)
    embed(1, SLAB + 1, near[0, ROW_AT : ROW_AT + 1], (volt, source))
    sweep(scal, OUTER, even, odd, absorb, source)
    for u in range(SLAB):
        msg[u] = even[OFF + OWN + u, PAD : PAD + ROWS]
    msg[SLAB, 0:HEART] = held[0]
    msg[SLAB, HEART : 2 * HEART] = held[SLAB - 1]
    msg[SLAB, 2 * HEART : ROWS] = jnp.zeros((HEART, 128), jnp.float32)


def second_inner(scal, own, on, held, first, absorb, source, even, odd, volt, out, copy):
    def keep(u, carry):
        copy[u, 0:ROWS] = own[u]
        copy[u, ROWS : ROWS + HEART] = first[u, V1_AT : V1_AT + HEART]
        put_heart(volt, u + 1, held[u])
        return carry

    lax.fori_loop(0, SLAB, keep, 0)
    clear_edges(even, odd)
    take(own, OWN, 1, even)
    take(on, END - 1, -1, even)
    put_heart(volt, SLAB + 1, on[SLAB, HEART : 2 * HEART])
    settle(1, SLAB, scal[3], even, volt, out)
    sweep(scal, INNER, even, odd, absorb, source)


def second_left(scal, near, absorb, source, *refs):
    even, odd, volt, out = refs[4:]
    take(near, OWN - 1, -1, even)
    put_heart(volt, 0, near[SLAB, 0:HEART])

    @pl.when(scal[4] == OWN)
    def _():
        volt[0] = volt[1]

    settle(0, 1, scal[3], even, volt, out)
    sweep(scal, LEFT, even, odd, absorb, source)


def second_right(scal, on2, absorb, source, *refs):
    even, odd = refs[2:]
    take(on2, END, 1, even)
    sweep(scal, RIGHT, even, odd, absorb, source)


def second_outer(scal, far, near, absorb, voltage, *refs):
    outs, (even, odd, source, volt_1), (joined,) = refs[4:8], refs[8:12], refs[12:]
    take(far, 0, 1, even)

    def plane(u, carry):
        put_heart(volt_1, u, far[u, ROWS : ROWS + HEART])
        return carry

    lax.fori_loop(0, SLAB, plane, 0)
    embed(1, SLAB + 1, near[0, ROW_AT : ROW_AT + 1], (volt_1, source))
    sweep(scal, OUTER, even, odd, absorb, source)
    sec, flip = scal[0], scal[2]

    def give(u, carry):
        joined[u, 0:ROWS] = even[OFF + OWN + u, PAD : PAD + ROWS]
        joined[u, ROWS : ROWS + HEART] = voltage[u]
        x = jnp.where(flip == 1, SLAB - 1 - u, u)
        for number in range(4):
            at = pl.multiple_of((sec ^ number) * HEART, HEART)
            outs[number][x] = joined[u, pl.ds(at, HEART)]
        return carry

    lax.fori_loop(0, SLAB, give, 0)


def spread_kernel(scal, own, got_1, got_2, got_3, out):
    for number, ref in enumerate((own, got_1, got_2, got_3)):
        at = scal[6 + number] * SLAB
        for u in range(SLAB):
            out[at + u] = ref[u]


def chain(sections, bricks):
    order = []
    for brick in range(bricks):
        forward = (brick + brick // 4) % 2 == 1
        for step in range(sections):
            sec = step if forward else sections - 1 - step
            order.append(sec * bricks + brick)
    return order


VMEM = pl.BlockSpec(memory_space=pltpu.VMEM)
SMEM = pl.BlockSpec(memory_space=pltpu.SMEM)


def call(kernel, args, outs, planes, scratch=(), state=(), limit=20):
    arrays = [jax.ShapeDtypeStruct(shape, jnp.float32) for shape in outs]
    arrays += [jax.ShapeDtypeStruct(ref.shape, ref.dtype) for ref in state]
    return pl.pallas_call(
        kernel,
        out_shape=arrays,
        in_specs=[SMEM] + [VMEM] * (len(args) + len(state) - 1),
        out_specs=[VMEM] * len(arrays),
        scratch_shapes=[pltpu.VMEM(shape, jnp.float32) for shape in scratch],
        input_output_aliases={len(args) + n: len(outs) + n for n in range(len(state))},
        compiler_params=pltpu.CompilerParams(vmem_limit_bytes=limit << 20),
        cost_estimate=pl.CostEstimate(
            flops=planes * 200_000, bytes_accessed=planes * 100_000, transcendentals=0
        ),
    )(*args, *state)


def body(potentials, coefficient, recovery, excitable, row_of):
    pot, coef = potentials[0], coefficient[0]
    sections, bricks = lax.axis_size("sec"), lax.axis_size("brick")
    order = chain(sections, bricks)
    count = len(order)
    last = count - 1
    partner = [(order[i], order[i ^ 1]) for i in range(count)]
    facing = []
    for i in range(1, last, 2):
        facing += [(order[i], order[i + 1]), (order[i + 1], order[i])]
    beyond = [(order[i], order[i + 2]) for i in range(0, count - 2, 2)]
    beyond += [(order[i], order[i - 2]) for i in range(3, count, 2)]

    def across(number):
        return [(sec, sec ^ number) for sec in range(sections)]

    sec = lax.axis_index("sec")
    brick = lax.axis_index("brick")
    forward = (brick + brick // 4) % 2 == 1

    def chunk_of(section):
        return jnp.where(forward, section, sections - 1 - section)

    chunk = chunk_of(sec)
    place = brick * sections + chunk
    no_facing = (place == 0) | (place == last)
    partner_end = (place == 1) | (place == last - 1)
    scal = jnp.stack(
        [
            sec,
            chunk,
            chunk % 2,
            row_of[0],
            jnp.where(no_facing, OWN, 0),
            jnp.where(partner_end, OWN + 2 * SLAB, SLOTS),
        ]
        + [chunk_of(sec ^ number) for number in range(4)]
    ).astype(jnp.int32)

    got = []
    for number in (1, 2, 3):
        start = SLAB * chunk_of(sec ^ number)
        piece = jnp.stack(
            [
                lax.dynamic_slice_in_dim(pot, start, SLAB, 0),
                lax.dynamic_slice_in_dim(coef, start, SLAB, 0),
            ]
        )
        got.append(lax.ppermute(piece, "sec", across(number)))

    msg, aux = call(
        gather_kernel,
        (scal, pot, coef, recovery, excitable, *got),
        [(SLAB, MSG, 128), (3, SLAB, HEART, 128)],
        20,
        scratch=[(SLAB, 128, 128)],
    )

    phi = (SLOTS + 2, PHI_PAD, 128)
    wide = (SLOTS, ROWS, 128)
    volt = (SLOTS, V_PAD, 128)
    heart = (SLAB, HEART, 128)

    def move(value, pairs):
        return lax.ppermute(value, AXES, pairs)

    near_1 = move(msg, facing)
    on = move(msg, partner)
    *state, copy = call(
        first_inner,
        (scal, msg, on, aux),
        [phi, phi, wide, wide, wide, volt, volt, heart, (SLAB, FAR, 128)],
        56,
    )
    far = move(copy, beyond)
    on2 = move(near_1, partner)
    *state, held = call(first_left, (scal, near_1, aux), [], 64, state=state)
    even, odd, absorb, source, later, volt_0, volt_1 = call(
        first_right, (scal, on2), [], 64, state=state
    )
    message, _, _, absorb, _, _ = call(
        first_outer,
        (scal, far, near_1, held),
        [(SLAB + 1, ROWS, 128)],
        184,
        state=[even, odd, absorb, source, volt_0],
    )

    near = move(message, facing)
    on = move(message, partner)
    even, odd, volt_2, voltage, copy = call(
        second_inner,
        (scal, message, on, held, msg, absorb, later),
        [phi, phi, (SLAB + 2, V_PAD, 128), heart, (SLAB, ROWS + HEART, 128)],
        56,
    )
    far = move(copy, beyond)
    on2 = move(near, partner)
    even, odd, _, voltage = call(
        second_left, (scal, near, absorb, later), [], 64, state=[even, odd, volt_2, voltage]
    )
    even, odd = call(second_right, (scal, on2, absorb, later), [], 64, state=[even, odd])
    outs = call(
        second_outer,
        (scal, far, near_1, absorb, voltage),
        [heart] * 4,
        184,
        scratch=[(SLAB, 128, 128)],
        state=[even, odd, later, volt_1],
    )[:4]
    back = [outs[0]]
    for number in (1, 2, 3):
        back.append(lax.ppermute(outs[number], "sec", across(number)))
    (result,) = call(spread_kernel, (scal, *back), [(sections * SLAB, HEART, 128)], 5)
    return result[None]


def solution(mesh):
    in_specs = (
        P("sec", "brick", None, None),
        P("sec", "brick", None, None),
        P("brick", None, None),
        P("brick", None, None),
        P("brick"),
    )
    out_specs = P("sec", "brick", None, None)
    return jax.shard_map(body, mesh=mesh, in_specs=in_specs, out_specs=out_specs, check_vma=False)
```

```python
import jax
import jax.numpy as jnp
from jax import lax
from jax.experimental import pallas as pl
from jax.experimental.pallas import tpu as pltpu
from jax.sharding import PartitionSpec as P

SUBSTEPS = 8
SWEEPS = 16

coupling_gain = 0.1
ionic_timestep = 0.05
ionic_gain = 8.0
recovery_rate = 0.1
recovery_decay = 0.5
spectrum_low = 0.04
spectrum_high = 12.32

SLAB = 8
ROWS = 96
HEART = 32
SLOTS = 40
OWN = 16
OFF = 1
PAD = 8
PART = 16
PARTS = ROWS // PART
AXES = ("sec", "brick")
V0_AT, POT_ROWS = 96, 128
V1_AT, ROW_AT, COEF_ROWS = 96, 128, 136
FAR_ROWS = POT_ROWS + ROWS
PHI_PAD = 112
V_PAD = 48


def chebyshev_weights(count):
    center = 0.5 * (spectrum_high + spectrum_low)
    spread = 0.5 * (spectrum_high - spectrum_low)
    ratio = center / spread
    current = 1.0 / ratio
    weights = [(0.0, 1.0 / center)]
    for _ in range(count):
        following = 1.0 / (2.0 * ratio - current)
        weights.append((following * current, 2.0 * following / spread))
        current = following
    return weights


WEIGHTS = chebyshev_weights(SWEEPS - 1)
SHIFT = 6.0 - 0.5 * (spectrum_high + spectrum_low)


def ionic(voltage, recovery, threshold, active):
    for _ in range(SUBSTEPS):
        drive = ionic_gain * voltage * (voltage - threshold) * (1.0 - voltage) - recovery
        relax = recovery_rate * (voltage - recovery_decay * recovery)
        voltage = voltage + ionic_timestep * active * drive
        recovery = recovery + ionic_timestep * active * relax
    return voltage, recovery


def lanes(shape):
    return lax.broadcasted_iota(jnp.int32, shape, len(shape) - 1)


def side_sum_zero(value):
    lane = lanes(value.shape)
    before = jnp.where(lane == 0, 0.0, pltpu.roll(value, 1, 1))
    after = jnp.where(lane == 127, 0.0, pltpu.roll(value, 127, 1))
    return before + after


def side_sum_edge(value):
    lane = lanes(value.shape)
    before = jnp.where(lane == 0, value, pltpu.roll(value, 1, 1))
    after = jnp.where(lane == 127, value, pltpu.roll(value, 127, 1))
    return before + after


def heart_laplace(ref, x):
    here = ref[x, PAD : PAD + HEART]
    total = ref[x - 1, PAD : PAD + HEART] + ref[x + 1, PAD : PAD + HEART]
    total = total + ref[x, PAD - 1 : PAD - 1 + HEART] + ref[x, PAD + 1 : PAD + 1 + HEART]
    return total + side_sum_edge(here) - 6.0 * here


def put_heart(ref, x, value):
    ref[x, PAD : PAD + HEART] = value
    ref[x, PAD - 1 : PAD] = value[0:1]
    ref[x, PAD + HEART : PAD + HEART + 1] = value[HEART - 1 : HEART]


def torso_current(ref, x, row):
    at = PAD + HEART * row
    here = ref[x, at : at + HEART]
    total = ref[x - 1, at : at + HEART] + ref[x + 1, at : at + HEART]
    total = total + ref[x, at - 1 : at - 1 + HEART] + ref[x, at + 1 : at + 1 + HEART]
    return total + side_sum_zero(here) - 6.0 * here


def halves(value):
    high = value.astype(jnp.bfloat16)
    return high, (value - high.astype(jnp.float32)).astype(jnp.bfloat16)


def sweep(scal, plan, even, odd, absorb, source):
    accs = [pltpu.ACC(part % 2)((PART, 256), jnp.float32) for part in range(2 * PARTS)]
    pl.run_scoped(lambda *refs: sweep_with(scal, plan, even, odd, absorb, source, refs), *accs)


def sweep_with(scal, plan, even, odd, absorb, source, accs):
    accs = (accs[:PARTS], accs[PARTS:])
    low_end, high_end = scal[4], scal[5]
    row = lax.broadcasted_iota(jnp.int32, (256, 256), 0)
    column = lax.broadcasted_iota(jnp.int32, (256, 256), 1)
    same = (row >= 128) == (column >= 128)
    apart = jnp.abs(row - column)
    beside = ((same & (apart == 1)) | (apart == 128)).astype(jnp.bfloat16)
    none = jnp.zeros((PART, 256), jnp.bfloat16)
    for unit in range(2):
        pltpu.matmul_push_rhs(beside, 0, unit)
    for number, acc in enumerate(accs[0] + accs[1]):
        pltpu.matmul_acc_lhs(acc, none, load_staged_rhs=0 if number < 2 else None)
    for acc in accs[0] + accs[1]:
        pltpu.matmul_pop(acc)

    def place(number, pair):
        _, runs = plan[number]
        first, size = runs[0]
        x = first + 2 * pair
        if len(runs) == 1:
            return x
        skip = runs[1][0] - first - size
        if isinstance(pair, int):
            return x + (skip if 2 * pair >= size else 0)
        return x + jnp.where(2 * pair >= size, skip, 0)

    def begin(number, pair, acc):
        level = plan[number][0]
        src = even if level % 2 else odd
        x = place(number, pair) + OFF
        for part in range(PARTS):
            at, to = PAD + PART * part, PAD + PART * (part + 1)
            high_0, low_0 = halves(src[x, at:to])
            high_1, low_1 = halves(src[x + 1, at:to])
            pltpu.matmul_acc_lhs(acc[part], jnp.concatenate([high_0, high_1], 1))
            pltpu.matmul_acc_lhs(acc[part], jnp.concatenate([low_0, low_1], 1))

    def finish(number, pair, acc):
        level = plan[number][0]
        src, dst = (even, odd) if level % 2 else (odd, even)
        x = place(number, pair)
        keeps, pushes = [], []
        for plane in range(2):
            inside = (x + plane >= low_end) & (x + plane < high_end)
            keeps.append(jnp.where(inside, WEIGHTS[level - 1][0], 0.0).astype(jnp.float32))
            pushes.append(jnp.where(inside, WEIGHTS[level - 1][1], 0.0).astype(jnp.float32))
        for part in range(PARTS):
            start, stop = PART * part, PART * (part + 1)
            at, to = PAD + start, PAD + stop
            sums = pltpu.matmul_pop(acc[part])
            for plane in range(2):
                here = x + plane
                total = src[here + OFF - 1 + 2 * plane, at:to]
                total = total + (src[here + OFF, at - 1 : to - 1] + src[here + OFF, at + 1 : to + 1])
                total = total + source[here, start:stop]
                total = total - absorb[here, start:stop] * src[here + OFF, at:to]
                total = pushes[plane] * (total + sums[:, 128 * plane : 128 * (plane + 1)])
                if level > 1:
                    total = total - keeps[plane] * dst[here + OFF, at:to]
                dst[here + OFF, at:to] = total

    one, other = accs
    begin(0, 0, one)
    for number, (_, runs) in enumerate(plan):
        pairs = sum(size for _, size in runs) // 2
        steps = (pairs - 1) // 2

        def two_pairs(step, carry, number=number, one=one, other=other):
            begin(number, 2 * step + 1, other)
            finish(number, 2 * step, one)
            begin(number, 2 * step + 2, one)
            finish(number, 2 * step + 1, other)
            return carry

        if steps:
            lax.fori_loop(0, steps, two_pairs, 0)
        pair = 2 * steps
        if pairs - pair == 2:
            begin(number, pair + 1, other)
            finish(number, pair, one)
            pair, one, other = pair + 1, other, one
        following = number + 1 < len(plan)
        if following and pairs > 2:
            begin(number + 1, 0, other)
        finish(number, pair, one)
        if following and pairs <= 2:
            begin(number + 1, 0, other)
        one, other = other, one


END = OWN + 2 * SLAB
INNER = [(k, [(OWN + k, 2 * SLAB - 2 * k)]) for k in range(1, SLAB)]
LEFT = [(k, [(SLAB + k, SLAB)]) for k in range(1, SLAB + 1)]
RIGHT = [(k, [(END - k, SLAB)]) for k in range(1, SLAB + 1)]
OUTER = [(k, [(k, SLAB)]) for k in range(1, SLAB + 1)]
OUTER += [(k, [(k, SLOTS - 2 * k)]) for k in range(SLAB + 1, SWEEPS + 1)]


def clear_edges(even, odd):
    zero = jnp.zeros((PAD, 128), jnp.float32)

    def edge(x, carry):
        for ref in (even, odd):
            ref[x, 0:PAD] = zero
            ref[x, PAD + ROWS : PHI_PAD] = zero
        return carry

    lax.fori_loop(0, SLOTS + 2, edge, 0)


def collect(scal, own, got, u, out):
    sec, chunk, flip = scal[0], scal[1], scal[2]
    x = jnp.where(flip == 1, SLAB - 1 - u, u)
    for number, ref in enumerate((own, *got)):
        at = pl.multiple_of((sec ^ number) * HEART, HEART)
        out[u, pl.ds(at, HEART)] = ref[x]
    return SLAB * chunk + x


def gather_pot(scal, own, got_1, got_2, got_3, msg):
    def plane(u, carry):
        collect(scal, own, (got_1, got_2, got_3), u, msg)
        return carry

    lax.fori_loop(0, SLAB, plane, 0)


def gather_coef(scal, rec, exc, pot, own, got_1, got_2, got_3, msg, aux, deep):
    strip = jnp.full((8, 128), scal[3].astype(jnp.float32))

    def plane(u, carry):
        whole = collect(scal, own, (got_1, got_2, got_3), u, deep)
        msg[u, 0:ROWS] = deep[u, 0:ROWS]
        threshold = deep[u, ROWS : ROWS + HEART]
        active = exc[whole].astype(jnp.float32)
        voltage, recovery = ionic(pot[u, V0_AT : V0_AT + HEART], rec[whole], threshold, active)
        msg[u, V1_AT : V1_AT + HEART] = voltage
        msg[u, ROW_AT : ROW_AT + 8] = strip
        aux[0, u] = threshold
        aux[1, u] = recovery
        aux[2, u] = active
        return carry

    lax.fori_loop(0, SLAB, plane, 0)


def take(ref, first, step, even):
    def plane(u, carry):
        even[first + step * u + OFF, PAD : PAD + ROWS] = ref[u, 0:ROWS]
        return carry

    lax.fori_loop(0, SLAB, plane, 0)


def take_first(pot, coef, at, first, step, even, absorb, volt, volt_1=None):
    def plane(u, carry):
        x = first + step * u
        even[x + OFF, PAD : PAD + ROWS] = pot[u, 0:ROWS]
        absorb[x] = coef[u, at : at + ROWS] + SHIFT
        put_heart(volt, x, pot[u, V0_AT : V0_AT + HEART])
        if volt_1 is not None:
            put_heart(volt_1, x, coef[u, V1_AT : V1_AT + HEART])
        return carry

    lax.fori_loop(0, SLAB, plane, 0)


def embed(low, high, mark, *fields):
    mark = jnp.broadcast_to(mark, (HEART, 128))

    def plane(x, carry):
        for ref, out in fields:
            gain = heart_laplace(ref, x)
            for layer in range(3):
                out[x, layer * HEART : (layer + 1) * HEART] = jnp.where(mark == layer, gain, 0.0)
        return carry

    lax.fori_loop(low, high, plane, 0)


def on_layer(row, work):
    for layer in range(3):

        @pl.when(row == layer)
        def _():
            work(layer)


def couple(first, last, row, even, volt_1, aux, held):
    def work(layer):
        def plane(u, carry):
            x = OWN + u
            gain = heart_laplace(volt_1, x) + torso_current(even, x + OFF, layer)
            voltage = volt_1[x, PAD : PAD + HEART] + coupling_gain * gain
            held[u], _ = ionic(voltage, aux[1, u], aux[0, u], aux[2, u])
            return carry

        lax.fori_loop(first, last, plane, 0)

    on_layer(row, work)


def settle(first, last, row, even, volt, out):
    def work(layer):
        def plane(u, carry):
            gain = heart_laplace(volt, u + 1) + torso_current(even, OWN + OFF + u, layer)
            out[u] = volt[u + 1, PAD : PAD + HEART] + coupling_gain * gain
            return carry

        lax.fori_loop(first, last, plane, 0)

    on_layer(row, work)


def first_inner(scal, pot, coef, on_pot, on_coef, aux, *refs):
    even, odd, absorb, source, later, volt, volt_1, held, copy = refs

    def send(u, carry):
        copy[u, 0:POT_ROWS] = pot[u]
        copy[u, POT_ROWS:FAR_ROWS] = coef[u, 0:ROWS]
        return carry

    lax.fori_loop(0, SLAB, send, 0)
    clear_edges(even, odd)
    take_first(pot, coef, 0, OWN, 1, even, absorb, volt, volt_1)
    take_first(on_pot, on_coef, 0, END - 1, -1, even, absorb, volt, volt_1)
    row = jnp.full((1, 128), scal[3].astype(jnp.float32))
    embed(OWN + 1, END - 1, row, (volt, source), (volt_1, later))
    couple(1, SLAB, scal[3], even, volt_1, aux, held)
    sweep(scal, INNER, even, odd, absorb, source)


def first_left(scal, pot, coef, aux, *refs):
    even, odd, absorb, source, later, volt, volt_1, held = refs[8:]
    take_first(pot, coef, 0, OWN - 1, -1, even, absorb, volt, volt_1)

    @pl.when(scal[4] == OWN)
    def _():
        for ref in (volt, volt_1):
            ref[OWN - 1] = ref[OWN]

    row = jnp.full((1, 128), scal[3].astype(jnp.float32))
    fields = ((volt, source), (volt_1, later))
    embed(SLAB + 1, OWN, coef[0, ROW_AT : ROW_AT + 1], *fields)
    embed(OWN, OWN + 1, row, *fields)
    couple(0, 1, scal[3], even, volt_1, aux, held)
    sweep(scal, LEFT, even, odd, absorb, source)


def first_right(scal, pot, coef, *refs):
    even, odd, absorb, source, later, volt, volt_1 = refs[7:]
    take_first(pot, coef, 0, END, 1, even, absorb, volt, volt_1)

    @pl.when(scal[5] == END)
    def _():
        for ref in (volt, volt_1):
            ref[END] = ref[END - 1]

    row = jnp.full((1, 128), scal[3].astype(jnp.float32))
    fields = ((volt, source), (volt_1, later))
    embed(END - 1, END, row, *fields)
    embed(END, SLOTS - 1, coef[0, ROW_AT : ROW_AT + 1], *fields)
    sweep(scal, RIGHT, even, odd, absorb, source)


def first_outer(scal, far, near, held, *refs):
    msg, even, odd, absorb, source, volt = refs[5:]
    take_first(far, far, POT_ROWS, 0, 1, even, absorb, volt)
    embed(1, SLAB + 1, near[0, ROW_AT : ROW_AT + 1], (volt, source))
    sweep(scal, OUTER, even, odd, absorb, source)
    for u in range(SLAB):
        msg[u] = even[OFF + OWN + u, PAD : PAD + ROWS]
    msg[SLAB, 0:HEART] = held[0]
    msg[SLAB, HEART : 2 * HEART] = held[SLAB - 1]
    msg[SLAB, 2 * HEART : ROWS] = jnp.zeros((HEART, 128), jnp.float32)


def second_open(scal, own, on, held, first, even, odd, volt, out, copy):
    def keep(u, carry):
        copy[u, 0:ROWS] = own[u]
        copy[u, ROWS : ROWS + HEART] = first[u, V1_AT : V1_AT + HEART]
        put_heart(volt, u + 1, held[u])
        return carry

    lax.fori_loop(0, SLAB, keep, 0)
    clear_edges(even, odd)
    take(own, OWN, 1, even)
    take(on, END - 1, -1, even)
    put_heart(volt, SLAB + 1, on[SLAB, HEART : 2 * HEART])
    settle(1, SLAB, scal[3], even, volt, out)


def second_inner(scal, absorb, source, *refs):
    even, odd = refs[2:]
    sweep(scal, INNER, even, odd, absorb, source)


def second_left(scal, near, absorb, source, *refs):
    even, odd, volt, out = refs[4:]
    take(near, OWN - 1, -1, even)
    put_heart(volt, 0, near[SLAB, 0:HEART])

    @pl.when(scal[4] == OWN)
    def _():
        volt[0] = volt[1]

    settle(0, 1, scal[3], even, volt, out)
    sweep(scal, LEFT, even, odd, absorb, source)


def second_right(scal, on2, absorb, source, *refs):
    even, odd = refs[2:]
    take(on2, END, 1, even)
    sweep(scal, RIGHT, even, odd, absorb, source)


def second_outer(scal, far, near, absorb, voltage, *refs):
    outs, (even, odd, source, volt_1), (joined,) = refs[4:8], refs[8:12], refs[12:]
    take(far, 0, 1, even)

    def plane(u, carry):
        put_heart(volt_1, u, far[u, ROWS : ROWS + HEART])
        return carry

    lax.fori_loop(0, SLAB, plane, 0)
    embed(1, SLAB + 1, near[0, ROW_AT : ROW_AT + 1], (volt_1, source))
    sweep(scal, OUTER, even, odd, absorb, source)
    sec, flip = scal[0], scal[2]

    def give(u, carry):
        joined[u, 0:ROWS] = even[OFF + OWN + u, PAD : PAD + ROWS]
        joined[u, ROWS : ROWS + HEART] = voltage[u]
        x = jnp.where(flip == 1, SLAB - 1 - u, u)
        for number in range(4):
            at = pl.multiple_of((sec ^ number) * HEART, HEART)
            outs[number][x] = joined[u, pl.ds(at, HEART)]
        return carry

    lax.fori_loop(0, SLAB, give, 0)


def spread_kernel(scal, own, got_1, got_2, got_3, out):
    for number, ref in enumerate((own, got_1, got_2, got_3)):
        at = scal[6 + number] * SLAB
        for u in range(SLAB):
            out[at + u] = ref[u]


def chain(sections, bricks):
    order = []
    for brick in range(bricks):
        forward = (brick + brick // 4) % 2 == 1
        for step in range(sections):
            sec = step if forward else sections - 1 - step
            order.append(sec * bricks + brick)
    return order


VMEM = pl.BlockSpec(memory_space=pltpu.VMEM)
SMEM = pl.BlockSpec(memory_space=pltpu.SMEM)


def call(kernel, args, outs, planes, scratch=(), state=(), limit=20):
    arrays = [jax.ShapeDtypeStruct(shape, jnp.float32) for shape in outs]
    arrays += [jax.ShapeDtypeStruct(ref.shape, ref.dtype) for ref in state]
    return pl.pallas_call(
        kernel,
        out_shape=arrays,
        in_specs=[SMEM] + [VMEM] * (len(args) + len(state) - 1),
        out_specs=[VMEM] * len(arrays),
        scratch_shapes=[pltpu.VMEM(shape, jnp.float32) for shape in scratch],
        input_output_aliases={len(args) + n: len(outs) + n for n in range(len(state))},
        compiler_params=pltpu.CompilerParams(vmem_limit_bytes=limit << 20),
        cost_estimate=pl.CostEstimate(
            flops=planes * 200_000, bytes_accessed=planes * 100_000, transcendentals=0
        ),
    )(*args, *state)


def body(potentials, coefficient, recovery, excitable, row_of):
    pot, coef = potentials[0], coefficient[0]
    sections, bricks = lax.axis_size("sec"), lax.axis_size("brick")
    order = chain(sections, bricks)
    count = len(order)
    last = count - 1
    partner = [(order[i], order[i ^ 1]) for i in range(count)]
    facing = []
    for i in range(1, last, 2):
        facing += [(order[i], order[i + 1]), (order[i + 1], order[i])]
    beyond = [(order[i], order[i + 2]) for i in range(0, count - 2, 2)]
    beyond += [(order[i], order[i - 2]) for i in range(3, count, 2)]

    def across(number):
        return [(sec, sec ^ number) for sec in range(sections)]

    sec = lax.axis_index("sec")
    brick = lax.axis_index("brick")
    forward = (brick + brick // 4) % 2 == 1

    def chunk_of(section):
        return jnp.where(forward, section, sections - 1 - section)

    chunk = chunk_of(sec)
    place = brick * sections + chunk
    no_facing = (place == 0) | (place == last)
    partner_end = (place == 1) | (place == last - 1)
    scal = jnp.stack(
        [
            sec,
            chunk,
            chunk % 2,
            row_of[0],
            jnp.where(no_facing, OWN, 0),
            jnp.where(partner_end, OWN + 2 * SLAB, SLOTS),
        ]
        + [chunk_of(sec ^ number) for number in range(4)]
    ).astype(jnp.int32)

    def swapped(value):
        got = [lax.dynamic_slice_in_dim(value, SLAB * chunk, SLAB, 0)]
        for number in (1, 2, 3):
            piece = lax.dynamic_slice_in_dim(value, SLAB * chunk_of(sec ^ number), SLAB, 0)
            got.append(lax.ppermute(piece, "sec", across(number)))
        return got

    got_pot = swapped(pot)
    got_coef = swapped(coef)
    (msg_pot,) = call(gather_pot, (scal, *got_pot), [(SLAB, POT_ROWS, 128)], 10)
    msg_coef, aux = call(
        gather_coef,
        (scal, recovery, excitable, msg_pot, *got_coef),
        [(SLAB, COEF_ROWS, 128), (3, SLAB, HEART, 128)],
        20,
        scratch=[(SLAB, 128, 128)],
    )

    phi = (SLOTS + 2, PHI_PAD, 128)
    wide = (SLOTS, ROWS, 128)
    volt = (SLOTS, V_PAD, 128)
    heart = (SLAB, HEART, 128)

    def move(value, pairs):
        return lax.ppermute(value, AXES, pairs)

    near_pot = move(msg_pot, facing)
    near_coef = move(msg_coef, facing)
    on_pot = move(msg_pot, partner)
    on_coef = move(msg_coef, partner)
    *state, copy = call(
        first_inner,
        (scal, msg_pot, msg_coef, on_pot, on_coef, aux),
        [phi, phi, wide, wide, wide, volt, volt, heart, (SLAB, FAR_ROWS, 128)],
        56,
    )
    far = move(copy, beyond)
    on2_pot = move(near_pot, partner)
    on2_coef = move(near_coef, partner)
    *state, held = call(first_left, (scal, near_pot, near_coef, aux), [], 64, state=state)
    even, odd, absorb, source, later, volt_0, volt_1 = call(
        first_right, (scal, on2_pot, on2_coef), [], 64, state=state
    )
    message, _, _, absorb, _, _ = call(
        first_outer,
        (scal, far, near_coef, held),
        [(SLAB + 1, ROWS, 128)],
        184,
        state=[even, odd, absorb, source, volt_0],
    )

    near = move(message, facing)
    on = move(message, partner)
    even, odd, volt_2, voltage, copy = call(
        second_open,
        (scal, message, on, held, msg_coef),
        [phi, phi, (SLAB + 2, V_PAD, 128), heart, (SLAB, ROWS + HEART, 128)],
        20,
    )
    far = move(copy, beyond)
    even, odd = call(second_inner, (scal, absorb, later), [], 56, state=[even, odd])
    on2 = move(near, partner)
    even, odd, _, voltage = call(
        second_left, (scal, near, absorb, later), [], 64, state=[even, odd, volt_2, voltage]
    )
    even, odd = call(second_right, (scal, on2, absorb, later), [], 64, state=[even, odd])
    outs = call(
        second_outer,
        (scal, far, near_coef, absorb, voltage),
        [heart] * 4,
        184,
        scratch=[(SLAB, 128, 128)],
        state=[even, odd, later, volt_1],
    )[:4]
    back = [outs[0]]
    for number in (1, 2, 3):
        back.append(lax.ppermute(outs[number], "sec", across(number)))
    (result,) = call(spread_kernel, (scal, *back), [(sections * SLAB, HEART, 128)], 5)
    return result[None]


def solution(mesh):
    in_specs = (
        P("sec", "brick", None, None),
        P("sec", "brick", None, None),
        P("brick", None, None),
        P("brick", None, None),
        P("brick"),
    )
    out_specs = P("sec", "brick", None, None)
    return jax.shard_map(body, mesh=mesh, in_specs=in_specs, out_specs=out_specs, check_vma=False)
```

```python
import jax
import jax.numpy as jnp
from jax import lax
from jax.experimental import pallas as pl
from jax.experimental.pallas import tpu as pltpu
from jax.sharding import PartitionSpec as P

SUBSTEPS = 8
SWEEPS = 16

coupling_gain = 0.1
ionic_timestep = 0.05
ionic_gain = 8.0
recovery_rate = 0.1
recovery_decay = 0.5
spectrum_low = 0.04
spectrum_high = 12.32

SLAB = 8
ROWS = 96
HEART = 32
SLOTS = 40
OWN = 16
OFF = 1
PAD = 8
PART = 16
PARTS = ROWS // PART
AXES = ("sec", "brick")
V0_AT, POT_ROWS = 96, 128
V1_AT, ROW_AT, COEF_ROWS = 96, 128, 136
FAR_ROWS = POT_ROWS + ROWS
PHI_PAD = 112
V_PAD = 48


def chebyshev_weights(count):
    center = 0.5 * (spectrum_high + spectrum_low)
    spread = 0.5 * (spectrum_high - spectrum_low)
    ratio = center / spread
    current = 1.0 / ratio
    weights = [(0.0, 1.0 / center)]
    for _ in range(count):
        following = 1.0 / (2.0 * ratio - current)
        weights.append((following * current, 2.0 * following / spread))
        current = following
    return weights


WEIGHTS = chebyshev_weights(SWEEPS - 1)
SHIFT = 6.0 - 0.5 * (spectrum_high + spectrum_low)


def ionic(voltage, recovery, threshold, active):
    for _ in range(SUBSTEPS):
        drive = ionic_gain * voltage * (voltage - threshold) * (1.0 - voltage) - recovery
        relax = recovery_rate * (voltage - recovery_decay * recovery)
        voltage = voltage + ionic_timestep * active * drive
        recovery = recovery + ionic_timestep * active * relax
    return voltage, recovery


def lanes(shape):
    return lax.broadcasted_iota(jnp.int32, shape, len(shape) - 1)


def side_sum_zero(value):
    lane = lanes(value.shape)
    before = jnp.where(lane == 0, 0.0, pltpu.roll(value, 1, 1))
    after = jnp.where(lane == 127, 0.0, pltpu.roll(value, 127, 1))
    return before + after


def side_sum_edge(value):
    lane = lanes(value.shape)
    before = jnp.where(lane == 0, value, pltpu.roll(value, 1, 1))
    after = jnp.where(lane == 127, value, pltpu.roll(value, 127, 1))
    return before + after


def heart_laplace(ref, x):
    here = ref[x, PAD : PAD + HEART]
    total = ref[x - 1, PAD : PAD + HEART] + ref[x + 1, PAD : PAD + HEART]
    total = total + ref[x, PAD - 1 : PAD - 1 + HEART] + ref[x, PAD + 1 : PAD + 1 + HEART]
    return total + side_sum_edge(here) - 6.0 * here


def put_heart(ref, x, value):
    ref[x, PAD : PAD + HEART] = value
    ref[x, PAD - 1 : PAD] = value[0:1]
    ref[x, PAD + HEART : PAD + HEART + 1] = value[HEART - 1 : HEART]


def torso_current(ref, x, row):
    at = PAD + HEART * row
    here = ref[x, at : at + HEART]
    total = ref[x - 1, at : at + HEART] + ref[x + 1, at : at + HEART]
    total = total + ref[x, at - 1 : at - 1 + HEART] + ref[x, at + 1 : at + 1 + HEART]
    return total + side_sum_zero(here) - 6.0 * here


def halves(value):
    high = value.astype(jnp.bfloat16)
    return high, (value - high.astype(jnp.float32)).astype(jnp.bfloat16)


def sweep(scal, plan, even, odd, absorb, source):
    accs = [pltpu.ACC(part % 2)((PART, 256), jnp.float32) for part in range(2 * PARTS)]
    pl.run_scoped(lambda *refs: sweep_with(scal, plan, even, odd, absorb, source, refs), *accs)


def sweep_with(scal, plan, even, odd, absorb, source, accs):
    accs = (accs[:PARTS], accs[PARTS:])
    low_end, high_end = scal[4], scal[5]
    row = lax.broadcasted_iota(jnp.int32, (256, 256), 0)
    column = lax.broadcasted_iota(jnp.int32, (256, 256), 1)
    same = (row >= 128) == (column >= 128)
    apart = jnp.abs(row - column)
    beside = ((same & (apart == 1)) | (apart == 128)).astype(jnp.bfloat16)
    none = jnp.zeros((PART, 256), jnp.bfloat16)
    for unit in range(2):
        pltpu.matmul_push_rhs(beside, 0, unit)
    for number, acc in enumerate(accs[0] + accs[1]):
        pltpu.matmul_acc_lhs(acc, none, load_staged_rhs=0 if number < 2 else None)
    for acc in accs[0] + accs[1]:
        pltpu.matmul_pop(acc)

    def place(number, pair):
        _, runs = plan[number]
        first, size = runs[0]
        x = first + 2 * pair
        if len(runs) == 1:
            return x
        skip = runs[1][0] - first - size
        if isinstance(pair, int):
            return x + (skip if 2 * pair >= size else 0)
        return x + jnp.where(2 * pair >= size, skip, 0)

    def begin(number, pair, acc):
        level = plan[number][0]
        src = even if level % 2 else odd
        x = place(number, pair) + OFF
        for part in range(PARTS):
            at, to = PAD + PART * part, PAD + PART * (part + 1)
            high_0, low_0 = halves(src[x, at:to])
            high_1, low_1 = halves(src[x + 1, at:to])
            pltpu.matmul_acc_lhs(acc[part], jnp.concatenate([high_0, high_1], 1))
            pltpu.matmul_acc_lhs(acc[part], jnp.concatenate([low_0, low_1], 1))

    def finish(number, pair, acc):
        level = plan[number][0]
        src, dst = (even, odd) if level % 2 else (odd, even)
        x = place(number, pair)
        keeps, pushes = [], []
        for plane in range(2):
            inside = (x + plane >= low_end) & (x + plane < high_end)
            keeps.append(jnp.where(inside, WEIGHTS[level - 1][0], 0.0).astype(jnp.float32))
            pushes.append(jnp.where(inside, WEIGHTS[level - 1][1], 0.0).astype(jnp.float32))
        for part in range(PARTS):
            start, stop = PART * part, PART * (part + 1)
            at, to = PAD + start, PAD + stop
            sums = pltpu.matmul_pop(acc[part])
            for plane in range(2):
                here = x + plane
                total = src[here + OFF - 1 + 2 * plane, at:to]
                total = total + (src[here + OFF, at - 1 : to - 1] + src[here + OFF, at + 1 : to + 1])
                total = total + source[here, start:stop]
                total = total - absorb[here, start:stop] * src[here + OFF, at:to]
                total = pushes[plane] * (total + sums[:, 128 * plane : 128 * (plane + 1)])
                if level > 1:
                    total = total - keeps[plane] * dst[here + OFF, at:to]
                dst[here + OFF, at:to] = total

    one, other = accs
    begin(0, 0, one)
    for number, (_, runs) in enumerate(plan):
        pairs = sum(size for _, size in runs) // 2
        steps = (pairs - 1) // 2

        def two_pairs(step, carry, number=number, one=one, other=other):
            begin(number, 2 * step + 1, other)
            finish(number, 2 * step, one)
            begin(number, 2 * step + 2, one)
            finish(number, 2 * step + 1, other)
            return carry

        if steps:
            lax.fori_loop(0, steps, two_pairs, 0)
        pair = 2 * steps
        if pairs - pair == 2:
            begin(number, pair + 1, other)
            finish(number, pair, one)
            pair, one, other = pair + 1, other, one
        following = number + 1 < len(plan)
        if following and pairs > 2:
            begin(number + 1, 0, other)
        finish(number, pair, one)
        if following and pairs <= 2:
            begin(number + 1, 0, other)
        one, other = other, one


END = OWN + 2 * SLAB
INNER = [(k, [(OWN + k, 2 * SLAB - 2 * k)]) for k in range(1, SLAB)]
LEFT = [(k, [(SLAB + k, SLAB)]) for k in range(1, SLAB + 1)]
RIGHT = [(k, [(END - k, SLAB)]) for k in range(1, SLAB + 1)]
OUTER = [(k, [(k, SLAB)]) for k in range(1, SLAB + 1)]
OUTER += [(k, [(k, SLOTS - 2 * k)]) for k in range(SLAB + 1, SWEEPS + 1)]


def clear_edges(even, odd):
    zero = jnp.zeros((PAD, 128), jnp.float32)

    def edge(x, carry):
        for ref in (even, odd):
            ref[x, 0:PAD] = zero
            ref[x, PAD + ROWS : PHI_PAD] = zero
        return carry

    lax.fori_loop(0, SLOTS + 2, edge, 0)


def collect(scal, own, got, u, out):
    sec, chunk, flip = scal[0], scal[1], scal[2]
    x = jnp.where(flip == 1, SLAB - 1 - u, u)
    for number, ref in enumerate((own, *got)):
        at = pl.multiple_of((sec ^ number) * HEART, HEART)
        out[u, pl.ds(at, HEART)] = ref[x]
    return SLAB * chunk + x


def gather_pot(scal, own, got_1, got_2, got_3, msg):
    def plane(u, carry):
        collect(scal, own, (got_1, got_2, got_3), u, msg)
        return carry

    lax.fori_loop(0, SLAB, plane, 0)


def gather_coef(scal, rec, exc, pot, own, got_1, got_2, got_3, msg, aux, deep):
    strip = jnp.full((8, 128), scal[3].astype(jnp.float32))

    def plane(u, carry):
        whole = collect(scal, own, (got_1, got_2, got_3), u, deep)
        msg[u, 0:ROWS] = deep[u, 0:ROWS]
        threshold = deep[u, ROWS : ROWS + HEART]
        active = exc[whole].astype(jnp.float32)
        voltage, recovery = ionic(pot[u, V0_AT : V0_AT + HEART], rec[whole], threshold, active)
        msg[u, V1_AT : V1_AT + HEART] = voltage
        msg[u, ROW_AT : ROW_AT + 8] = strip
        aux[0, u] = threshold
        aux[1, u] = recovery
        aux[2, u] = active
        return carry

    lax.fori_loop(0, SLAB, plane, 0)


def take(ref, first, step, even):
    def plane(u, carry):
        even[first + step * u + OFF, PAD : PAD + ROWS] = ref[u, 0:ROWS]
        return carry

    lax.fori_loop(0, SLAB, plane, 0)


def take_first(pot, coef, at, first, step, even, absorb, volt, volt_1=None):
    def plane(u, carry):
        x = first + step * u
        even[x + OFF, PAD : PAD + ROWS] = pot[u, 0:ROWS]
        absorb[x] = coef[u, at : at + ROWS] + SHIFT
        put_heart(volt, x, pot[u, V0_AT : V0_AT + HEART])
        if volt_1 is not None:
            put_heart(volt_1, x, coef[u, V1_AT : V1_AT + HEART])
        return carry

    lax.fori_loop(0, SLAB, plane, 0)


def embed(low, high, mark, *fields):
    mark = jnp.broadcast_to(mark, (HEART, 128))

    def plane(x, carry):
        for ref, out in fields:
            gain = heart_laplace(ref, x)
            for layer in range(3):
                out[x, layer * HEART : (layer + 1) * HEART] = jnp.where(mark == layer, gain, 0.0)
        return carry

    lax.fori_loop(low, high, plane, 0)


def on_layer(row, work):
    for layer in range(3):

        @pl.when(row == layer)
        def _():
            work(layer)


def couple(first, last, row, even, volt_1, aux, held):
    def work(layer):
        def plane(u, carry):
            x = OWN + u
            gain = heart_laplace(volt_1, x) + torso_current(even, x + OFF, layer)
            voltage = volt_1[x, PAD : PAD + HEART] + coupling_gain * gain
            held[u], _ = ionic(voltage, aux[1, u], aux[0, u], aux[2, u])
            return carry

        lax.fori_loop(first, last, plane, 0)

    on_layer(row, work)


def settle(first, last, row, even, volt, out):
    def work(layer):
        def plane(u, carry):
            gain = heart_laplace(volt, u + 1) + torso_current(even, OWN + OFF + u, layer)
            out[u] = volt[u + 1, PAD : PAD + HEART] + coupling_gain * gain
            return carry

        lax.fori_loop(first, last, plane, 0)

    on_layer(row, work)


def first_open(scal, pot, coef, copy):
    def send(u, carry):
        copy[u, 0:POT_ROWS] = pot[u]
        copy[u, POT_ROWS:FAR_ROWS] = coef[u, 0:ROWS]
        return carry

    lax.fori_loop(0, SLAB, send, 0)


def first_inner(scal, pot, coef, on_pot, on_coef, aux, *refs):
    even, odd, absorb, source, later, volt, volt_1, held = refs
    clear_edges(even, odd)
    take_first(pot, coef, 0, OWN, 1, even, absorb, volt, volt_1)
    take_first(on_pot, on_coef, 0, END - 1, -1, even, absorb, volt, volt_1)
    row = jnp.full((1, 128), scal[3].astype(jnp.float32))
    embed(OWN + 1, END - 1, row, (volt, source), (volt_1, later))
    couple(1, SLAB, scal[3], even, volt_1, aux, held)
    sweep(scal, INNER, even, odd, absorb, source)


def first_left(scal, pot, coef, aux, *refs):
    even, odd, absorb, source, later, volt, volt_1, held = refs[8:]
    take_first(pot, coef, 0, OWN - 1, -1, even, absorb, volt, volt_1)

    @pl.when(scal[4] == OWN)
    def _():
        for ref in (volt, volt_1):
            ref[OWN - 1] = ref[OWN]

    row = jnp.full((1, 128), scal[3].astype(jnp.float32))
    fields = ((volt, source), (volt_1, later))
    embed(SLAB + 1, OWN, coef[0, ROW_AT : ROW_AT + 1], *fields)
    embed(OWN, OWN + 1, row, *fields)
    couple(0, 1, scal[3], even, volt_1, aux, held)
    sweep(scal, LEFT, even, odd, absorb, source)


def first_right(scal, pot, coef, *refs):
    even, odd, absorb, source, later, volt, volt_1 = refs[7:]
    take_first(pot, coef, 0, END, 1, even, absorb, volt, volt_1)

    @pl.when(scal[5] == END)
    def _():
        for ref in (volt, volt_1):
            ref[END] = ref[END - 1]

    row = jnp.full((1, 128), scal[3].astype(jnp.float32))
    fields = ((volt, source), (volt_1, later))
    embed(END - 1, END, row, *fields)
    embed(END, SLOTS - 1, coef[0, ROW_AT : ROW_AT + 1], *fields)
    sweep(scal, RIGHT, even, odd, absorb, source)


def first_outer(scal, far, near, held, *refs):
    msg, even, odd, absorb, source, volt = refs[5:]
    take_first(far, far, POT_ROWS, 0, 1, even, absorb, volt)
    embed(1, SLAB + 1, near[0, ROW_AT : ROW_AT + 1], (volt, source))
    sweep(scal, OUTER, even, odd, absorb, source)
    for u in range(SLAB):
        msg[u] = even[OFF + OWN + u, PAD : PAD + ROWS]
    msg[SLAB, 0:HEART] = held[0]
    msg[SLAB, HEART : 2 * HEART] = held[SLAB - 1]
    msg[SLAB, 2 * HEART : ROWS] = jnp.zeros((HEART, 128), jnp.float32)


def second_open(scal, own, on, held, first, even, odd, volt, out, copy):
    def keep(u, carry):
        copy[u, 0:ROWS] = own[u]
        copy[u, ROWS : ROWS + HEART] = first[u, V1_AT : V1_AT + HEART]
        put_heart(volt, u + 1, held[u])
        return carry

    lax.fori_loop(0, SLAB, keep, 0)
    clear_edges(even, odd)
    take(own, OWN, 1, even)
    take(on, END - 1, -1, even)
    put_heart(volt, SLAB + 1, on[SLAB, HEART : 2 * HEART])
    settle(1, SLAB, scal[3], even, volt, out)


def second_inner(scal, absorb, source, *refs):
    even, odd = refs[2:]
    sweep(scal, INNER, even, odd, absorb, source)


def second_left(scal, near, absorb, source, *refs):
    even, odd, volt, out = refs[4:]
    take(near, OWN - 1, -1, even)
    put_heart(volt, 0, near[SLAB, 0:HEART])

    @pl.when(scal[4] == OWN)
    def _():
        volt[0] = volt[1]

    settle(0, 1, scal[3], even, volt, out)
    sweep(scal, LEFT, even, odd, absorb, source)


def second_right(scal, on2, absorb, source, *refs):
    even, odd = refs[2:]
    take(on2, END, 1, even)
    sweep(scal, RIGHT, even, odd, absorb, source)


def second_outer(scal, far, near, absorb, voltage, *refs):
    outs, (even, odd, source, volt_1), (joined,) = refs[4:8], refs[8:12], refs[12:]
    take(far, 0, 1, even)

    def plane(u, carry):
        put_heart(volt_1, u, far[u, ROWS : ROWS + HEART])
        return carry

    lax.fori_loop(0, SLAB, plane, 0)
    embed(1, SLAB + 1, near[0, ROW_AT : ROW_AT + 1], (volt_1, source))
    sweep(scal, OUTER, even, odd, absorb, source)
    sec, flip = scal[0], scal[2]

    def give(u, carry):
        joined[u, 0:ROWS] = even[OFF + OWN + u, PAD : PAD + ROWS]
        joined[u, ROWS : ROWS + HEART] = voltage[u]
        x = jnp.where(flip == 1, SLAB - 1 - u, u)
        for number in range(4):
            at = pl.multiple_of((sec ^ number) * HEART, HEART)
            outs[number][x] = joined[u, pl.ds(at, HEART)]
        return carry

    lax.fori_loop(0, SLAB, give, 0)


def spread_kernel(scal, own, got_1, got_2, got_3, out):
    for number, ref in enumerate((own, got_1, got_2, got_3)):
        at = scal[6 + number] * SLAB
        for u in range(SLAB):
            out[at + u] = ref[u]


def chain(sections, bricks):
    order = []
    for brick in range(bricks):
        forward = (brick + brick // 4) % 2 == 1
        for step in range(sections):
            sec = step if forward else sections - 1 - step
            order.append(sec * bricks + brick)
    return order


VMEM = pl.BlockSpec(memory_space=pltpu.VMEM)
SMEM = pl.BlockSpec(memory_space=pltpu.SMEM)


def call(kernel, args, outs, planes, scratch=(), state=(), limit=20):
    arrays = [jax.ShapeDtypeStruct(shape, jnp.float32) for shape in outs]
    arrays += [jax.ShapeDtypeStruct(ref.shape, ref.dtype) for ref in state]
    return pl.pallas_call(
        kernel,
        out_shape=arrays,
        in_specs=[SMEM] + [VMEM] * (len(args) + len(state) - 1),
        out_specs=[VMEM] * len(arrays),
        scratch_shapes=[pltpu.VMEM(shape, jnp.float32) for shape in scratch],
        input_output_aliases={len(args) + n: len(outs) + n for n in range(len(state))},
        compiler_params=pltpu.CompilerParams(vmem_limit_bytes=limit << 20),
        cost_estimate=pl.CostEstimate(
            flops=planes * 200_000, bytes_accessed=planes * 100_000, transcendentals=0
        ),
    )(*args, *state)


def body(potentials, coefficient, recovery, excitable, row_of):
    pot, coef = potentials[0], coefficient[0]
    sections, bricks = lax.axis_size("sec"), lax.axis_size("brick")
    order = chain(sections, bricks)
    count = len(order)
    last = count - 1
    partner = [(order[i], order[i ^ 1]) for i in range(count)]
    facing = []
    for i in range(1, last, 2):
        facing += [(order[i], order[i + 1]), (order[i + 1], order[i])]
    beyond = [(order[i], order[i + 2]) for i in range(0, count - 2, 2)]
    beyond += [(order[i], order[i - 2]) for i in range(3, count, 2)]

    def across(number):
        return [(sec, sec ^ number) for sec in range(sections)]

    sec = lax.axis_index("sec")
    brick = lax.axis_index("brick")
    forward = (brick + brick // 4) % 2 == 1

    def chunk_of(section):
        return jnp.where(forward, section, sections - 1 - section)

    chunk = chunk_of(sec)
    place = brick * sections + chunk
    no_facing = (place == 0) | (place == last)
    partner_end = (place == 1) | (place == last - 1)
    scal = jnp.stack(
        [
            sec,
            chunk,
            chunk % 2,
            row_of[0],
            jnp.where(no_facing, OWN, 0),
            jnp.where(partner_end, OWN + 2 * SLAB, SLOTS),
        ]
        + [chunk_of(sec ^ number) for number in range(4)]
    ).astype(jnp.int32)

    def swapped(value):
        got = [lax.dynamic_slice_in_dim(value, SLAB * chunk, SLAB, 0)]
        for number in (1, 2, 3):
            piece = lax.dynamic_slice_in_dim(value, SLAB * chunk_of(sec ^ number), SLAB, 0)
            got.append(lax.ppermute(piece, "sec", across(number)))
        return got

    got_pot = swapped(pot)
    got_coef = swapped(coef)
    (msg_pot,) = call(gather_pot, (scal, *got_pot), [(SLAB, POT_ROWS, 128)], 10)
    msg_coef, aux = call(
        gather_coef,
        (scal, recovery, excitable, msg_pot, *got_coef),
        [(SLAB, COEF_ROWS, 128), (3, SLAB, HEART, 128)],
        20,
        scratch=[(SLAB, 128, 128)],
    )

    phi = (SLOTS + 2, PHI_PAD, 128)
    wide = (SLOTS, ROWS, 128)
    volt = (SLOTS, V_PAD, 128)
    heart = (SLAB, HEART, 128)

    def move(value, pairs):
        return lax.ppermute(value, AXES, pairs)

    near_pot = move(msg_pot, facing)
    near_coef = move(msg_coef, facing)
    on_pot = move(msg_pot, partner)
    on_coef = move(msg_coef, partner)
    (copy,) = call(first_open, (scal, msg_pot, msg_coef), [(SLAB, FAR_ROWS, 128)], 5)
    far = move(copy, beyond)
    state = call(
        first_inner,
        (scal, msg_pot, msg_coef, on_pot, on_coef, aux),
        [phi, phi, wide, wide, wide, volt, volt, heart],
        56,
    )
    on2_pot = move(near_pot, partner)
    on2_coef = move(near_coef, partner)
    *state, held = call(first_left, (scal, near_pot, near_coef, aux), [], 64, state=state)
    even, odd, absorb, source, later, volt_0, volt_1 = call(
        first_right, (scal, on2_pot, on2_coef), [], 64, state=state
    )
    message, _, _, absorb, _, _ = call(
        first_outer,
        (scal, far, near_coef, held),
        [(SLAB + 1, ROWS, 128)],
        184,
        state=[even, odd, absorb, source, volt_0],
    )

    near = move(message, facing)
    on = move(message, partner)
    even, odd, volt_2, voltage, copy = call(
        second_open,
        (scal, message, on, held, msg_coef),
        [phi, phi, (SLAB + 2, V_PAD, 128), heart, (SLAB, ROWS + HEART, 128)],
        20,
    )
    far = move(copy, beyond)
    even, odd = call(second_inner, (scal, absorb, later), [], 56, state=[even, odd])
    on2 = move(near, partner)
    even, odd, _, voltage = call(
        second_left, (scal, near, absorb, later), [], 64, state=[even, odd, volt_2, voltage]
    )
    even, odd = call(second_right, (scal, on2, absorb, later), [], 64, state=[even, odd])
    outs = call(
        second_outer,
        (scal, far, near_coef, absorb, voltage),
        [heart] * 4,
        184,
        scratch=[(SLAB, 128, 128)],
        state=[even, odd, later, volt_1],
    )[:4]
    back = [outs[0]]
    for number in (1, 2, 3):
        back.append(lax.ppermute(outs[number], "sec", across(number)))
    (result,) = call(spread_kernel, (scal, *back), [(sections * SLAB, HEART, 128)], 5)
    return result[None]


def solution(mesh):
    in_specs = (
        P("sec", "brick", None, None),
        P("sec", "brick", None, None),
        P("brick", None, None),
        P("brick", None, None),
        P("brick"),
    )
    out_specs = P("sec", "brick", None, None)
    return jax.shard_map(body, mesh=mesh, in_specs=in_specs, out_specs=out_specs, check_vma=False)
```

```python
import jax
import jax.numpy as jnp
from jax import lax
from jax.experimental import pallas as pl
from jax.experimental.pallas import tpu as pltpu
from jax.sharding import PartitionSpec as P

SUBSTEPS = 8
SWEEPS = 16

coupling_gain = 0.1
ionic_timestep = 0.05
ionic_gain = 8.0
recovery_rate = 0.1
recovery_decay = 0.5
spectrum_low = 0.04
spectrum_high = 12.32

SLAB = 8
ROWS = 96
HEART = 32
SLOTS = 40
OWN = 16
OFF = 1
PAD = 8
PART = 16
PARTS = ROWS // PART
AXES = ("sec", "brick")
V0_AT, POT_ROWS = 96, 128
V1_AT, ROW_AT, COEF_ROWS = 96, 128, 136
FAR_ROWS = POT_ROWS + ROWS
PHI_PAD = 112
V_PAD = 48


CENTER = 0.5 * (spectrum_high + spectrum_low)
SPREAD = 0.5 * (spectrum_high - spectrum_low)


def chebyshev_polynomials(count):
    ratio = CENTER / SPREAD
    values = [1.0, ratio]
    while len(values) <= count:
        values.append(2.0 * ratio * values[-1] - values[-2])
    return values


SCALES = chebyshev_polynomials(SWEEPS)
SHIFT = 6.0 - CENTER


def ionic(voltage, recovery, threshold, active):
    for _ in range(SUBSTEPS):
        drive = ionic_gain * voltage * (voltage - threshold) * (1.0 - voltage) - recovery
        relax = recovery_rate * (voltage - recovery_decay * recovery)
        voltage = voltage + ionic_timestep * active * drive
        recovery = recovery + ionic_timestep * active * relax
    return voltage, recovery


def lanes(shape):
    return lax.broadcasted_iota(jnp.int32, shape, len(shape) - 1)


def side_sum_zero(value):
    lane = lanes(value.shape)
    before = jnp.where(lane == 0, 0.0, pltpu.roll(value, 1, 1))
    after = jnp.where(lane == 127, 0.0, pltpu.roll(value, 127, 1))
    return before + after


def side_sum_edge(value):
    lane = lanes(value.shape)
    before = jnp.where(lane == 0, value, pltpu.roll(value, 1, 1))
    after = jnp.where(lane == 127, value, pltpu.roll(value, 127, 1))
    return before + after


def heart_laplace(ref, x):
    here = ref[x, PAD : PAD + HEART]
    total = ref[x - 1, PAD : PAD + HEART] + ref[x + 1, PAD : PAD + HEART]
    total = total + ref[x, PAD - 1 : PAD - 1 + HEART] + ref[x, PAD + 1 : PAD + 1 + HEART]
    return total + side_sum_edge(here) - 6.0 * here


def put_heart(ref, x, value):
    ref[x, PAD : PAD + HEART] = value
    ref[x, PAD - 1 : PAD] = value[0:1]
    ref[x, PAD + HEART : PAD + HEART + 1] = value[HEART - 1 : HEART]


def torso_current(ref, x, row):
    at = PAD + HEART * row
    here = ref[x, at : at + HEART]
    total = ref[x - 1, at : at + HEART] + ref[x + 1, at : at + HEART]
    total = total + ref[x, at - 1 : at - 1 + HEART] + ref[x, at + 1 : at + 1 + HEART]
    return total + side_sum_zero(here) - 6.0 * here


def halves(value):
    high = value.astype(jnp.bfloat16)
    return high, (value - high.astype(jnp.float32)).astype(jnp.bfloat16)


def sweep(scal, plan, even, odd, absorb, source, rows):
    accs = [pltpu.ACC(part % 2)((PART, 256), jnp.float32) for part in range(2 * PARTS)]
    pl.run_scoped(
        lambda *refs: sweep_with(scal, plan, even, odd, absorb, source, rows, refs), *accs
    )


def row_mark(ref):
    return jnp.max(ref[0, ROW_AT : ROW_AT + 8]).astype(jnp.int32)


def sweep_with(scal, plan, even, odd, absorb, source, rows, accs):
    accs = (accs[:PARTS], accs[PARTS:])
    low_end, high_end = scal[4], scal[5]
    row = lax.broadcasted_iota(jnp.int32, (256, 256), 0)
    column = lax.broadcasted_iota(jnp.int32, (256, 256), 1)
    same = (row >= 128) == (column >= 128)
    apart = jnp.abs(row - column)
    beside = ((same & (apart == 1)) | (apart == 128)).astype(jnp.bfloat16)
    none = jnp.zeros((PART, 256), jnp.bfloat16)
    for unit in range(2):
        pltpu.matmul_push_rhs(beside, 0, unit)
    for number, acc in enumerate(accs[0] + accs[1]):
        pltpu.matmul_acc_lhs(acc, none, load_staged_rhs=0 if number < 2 else None)
    for acc in accs[0] + accs[1]:
        pltpu.matmul_pop(acc)

    def place(number, pair):
        _, runs = plan[number]
        first, size = runs[0]
        x = first + 2 * pair
        if len(runs) == 1:
            return x
        skip = runs[1][0] - first - size
        if isinstance(pair, int):
            return x + (skip if 2 * pair >= size else 0)
        return x + jnp.where(2 * pair >= size, skip, 0)

    def weight(level, x):
        inside = (x >= low_end) & (x < high_end)
        push = (1.0 if level == 1 else 2.0) / SPREAD
        return jnp.where(inside, push, 0.0).astype(jnp.float32)

    def begin(number, pair, acc):
        level = plan[number][0]
        src, dst = (even, odd) if level % 2 else (odd, even)
        x = place(number, pair)
        if level > 1:
            for plane in range(2):
                here = x + plane
                at = pl.multiple_of(rows(here) * HEART, HEART)
                to = pl.multiple_of(rows(here) * HEART + PAD, PAD)
                part = weight(level, here) * SCALES[level - 1] * source[here, pl.ds(at, HEART)]
                dst[here + OFF, pl.ds(to, HEART)] = dst[here + OFF, pl.ds(to, HEART)] - part
        x = x + OFF
        for part in range(PARTS):
            at, to = PAD + PART * part, PAD + PART * (part + 1)
            high_0, low_0 = halves(src[x, at:to])
            high_1, low_1 = halves(src[x + 1, at:to])
            pltpu.matmul_acc_lhs(acc[part], jnp.concatenate([high_0, high_1], 1))
            pltpu.matmul_acc_lhs(acc[part], jnp.concatenate([low_0, low_1], 1))

    def finish(number, pair, acc):
        level = plan[number][0]
        src, dst = (even, odd) if level % 2 else (odd, even)
        x = place(number, pair)
        pushes = [weight(level, x + plane) for plane in range(2)]
        for part in range(PARTS):
            start, stop = PART * part, PART * (part + 1)
            at, to = PAD + start, PAD + stop
            sums = pltpu.matmul_pop(acc[part])
            for plane in range(2):
                here = x + plane
                total = src[here + OFF - 1 + 2 * plane, at:to]
                total = total + (src[here + OFF, at - 1 : to - 1] + src[here + OFF, at + 1 : to + 1])
                if level == 1:
                    total = total + source[here, start:stop]
                total = total - absorb[here, start:stop] * src[here + OFF, at:to]
                total = pushes[plane] * (total + sums[:, 128 * plane : 128 * (plane + 1)])
                if level > 1:
                    total = total - dst[here + OFF, at:to]
                dst[here + OFF, at:to] = total

    one, other = accs
    begin(0, 0, one)
    for number, (_, runs) in enumerate(plan):
        pairs = sum(size for _, size in runs) // 2
        steps = (pairs - 1) // 2

        def two_pairs(step, carry, number=number, one=one, other=other):
            begin(number, 2 * step + 1, other)
            finish(number, 2 * step, one)
            begin(number, 2 * step + 2, one)
            finish(number, 2 * step + 1, other)
            return carry

        if steps:
            lax.fori_loop(0, steps, two_pairs, 0)
        pair = 2 * steps
        if pairs - pair == 2:
            begin(number, pair + 1, other)
            finish(number, pair, one)
            pair, one, other = pair + 1, other, one
        following = number + 1 < len(plan)
        if following and pairs > 2:
            begin(number + 1, 0, other)
        finish(number, pair, one)
        if following and pairs <= 2:
            begin(number + 1, 0, other)
        one, other = other, one


END = OWN + 2 * SLAB
INNER = [(k, [(OWN + k, 2 * SLAB - 2 * k)]) for k in range(1, SLAB)]
LEFT = [(k, [(SLAB + k, SLAB)]) for k in range(1, SLAB + 1)]
RIGHT = [(k, [(END - k, SLAB)]) for k in range(1, SLAB + 1)]
OUTER = [(k, [(k, SLAB)]) for k in range(1, SLAB + 1)]
OUTER += [(k, [(k, SLOTS - 2 * k)]) for k in range(SLAB + 1, SWEEPS + 1)]


def clear_edges(even, odd):
    zero = jnp.zeros((PAD, 128), jnp.float32)

    def edge(x, carry):
        for ref in (even, odd):
            ref[x, 0:PAD] = zero
            ref[x, PAD + ROWS : PHI_PAD] = zero
        return carry

    lax.fori_loop(0, SLOTS + 2, edge, 0)


def collect(scal, own, got, u, out):
    sec, chunk, flip = scal[0], scal[1], scal[2]
    x = jnp.where(flip == 1, SLAB - 1 - u, u)
    for number, ref in enumerate((own, *got)):
        at = pl.multiple_of((sec ^ number) * HEART, HEART)
        out[u, pl.ds(at, HEART)] = ref[x]
    return SLAB * chunk + x


def gather_pot(scal, own, got_1, got_2, got_3, msg):
    def plane(u, carry):
        collect(scal, own, (got_1, got_2, got_3), u, msg)
        return carry

    lax.fori_loop(0, SLAB, plane, 0)


def gather_coef(scal, rec, exc, pot, own, got_1, got_2, got_3, msg, aux, deep):
    strip = jnp.full((8, 128), scal[3].astype(jnp.float32))

    def plane(u, carry):
        whole = collect(scal, own, (got_1, got_2, got_3), u, deep)
        msg[u, 0:ROWS] = deep[u, 0:ROWS]
        threshold = deep[u, ROWS : ROWS + HEART]
        active = exc[whole].astype(jnp.float32)
        voltage, recovery = ionic(pot[u, V0_AT : V0_AT + HEART], rec[whole], threshold, active)
        msg[u, V1_AT : V1_AT + HEART] = voltage
        msg[u, ROW_AT : ROW_AT + 8] = strip
        aux[0, u] = threshold
        aux[1, u] = recovery
        aux[2, u] = active
        return carry

    lax.fori_loop(0, SLAB, plane, 0)


def take(ref, first, step, even):
    def plane(u, carry):
        even[first + step * u + OFF, PAD : PAD + ROWS] = ref[u, 0:ROWS]
        return carry

    lax.fori_loop(0, SLAB, plane, 0)


def take_first(pot, coef, at, first, step, even, absorb, volt, volt_1=None):
    def plane(u, carry):
        x = first + step * u
        even[x + OFF, PAD : PAD + ROWS] = pot[u, 0:ROWS]
        absorb[x] = coef[u, at : at + ROWS] + SHIFT
        put_heart(volt, x, pot[u, V0_AT : V0_AT + HEART])
        if volt_1 is not None:
            put_heart(volt_1, x, coef[u, V1_AT : V1_AT + HEART])
        return carry

    lax.fori_loop(0, SLAB, plane, 0)


def embed(low, high, mark, *fields):
    mark = jnp.broadcast_to(mark, (HEART, 128))

    def plane(x, carry):
        for ref, out in fields:
            gain = heart_laplace(ref, x)
            for layer in range(3):
                out[x, layer * HEART : (layer + 1) * HEART] = jnp.where(mark == layer, gain, 0.0)
        return carry

    lax.fori_loop(low, high, plane, 0)


def on_layer(row, work):
    for layer in range(3):

        @pl.when(row == layer)
        def _():
            work(layer)


def couple(first, last, row, even, volt_1, aux, held):
    def work(layer):
        def plane(u, carry):
            x = OWN + u
            gain = heart_laplace(volt_1, x) + torso_current(even, x + OFF, layer)
            voltage = volt_1[x, PAD : PAD + HEART] + coupling_gain * gain
            held[u], _ = ionic(voltage, aux[1, u], aux[0, u], aux[2, u])
            return carry

        lax.fori_loop(first, last, plane, 0)

    on_layer(row, work)


def settle(first, last, row, even, volt, out):
    def work(layer):
        def plane(u, carry):
            gain = heart_laplace(volt, u + 1) + torso_current(even, OWN + OFF + u, layer)
            out[u] = volt[u + 1, PAD : PAD + HEART] + coupling_gain * gain
            return carry

        lax.fori_loop(first, last, plane, 0)

    on_layer(row, work)


def first_open(scal, pot, coef, copy):
    def send(u, carry):
        copy[u, 0:POT_ROWS] = pot[u]
        copy[u, POT_ROWS:FAR_ROWS] = coef[u, 0:ROWS]
        return carry

    lax.fori_loop(0, SLAB, send, 0)


def first_inner(scal, pot, coef, on_pot, on_coef, aux, *refs):
    even, odd, absorb, source, later, volt, volt_1, held = refs
    clear_edges(even, odd)
    take_first(pot, coef, 0, OWN, 1, even, absorb, volt, volt_1)
    take_first(on_pot, on_coef, 0, END - 1, -1, even, absorb, volt, volt_1)
    row = jnp.full((1, 128), scal[3].astype(jnp.float32))
    embed(OWN + 1, END - 1, row, (volt, source), (volt_1, later))
    couple(1, SLAB, scal[3], even, volt_1, aux, held)
    sweep(scal, INNER, even, odd, absorb, source, lambda x: scal[3])


def first_left(scal, pot, coef, aux, *refs):
    even, odd, absorb, source, later, volt, volt_1, held = refs[8:]
    take_first(pot, coef, 0, OWN - 1, -1, even, absorb, volt, volt_1)

    @pl.when(scal[4] == OWN)
    def _():
        for ref in (volt, volt_1):
            ref[OWN - 1] = ref[OWN]

    row = jnp.full((1, 128), scal[3].astype(jnp.float32))
    fields = ((volt, source), (volt_1, later))
    embed(SLAB + 1, OWN, coef[0, ROW_AT : ROW_AT + 1], *fields)
    embed(OWN, OWN + 1, row, *fields)
    couple(0, 1, scal[3], even, volt_1, aux, held)
    near_row = row_mark(coef)
    sweep(scal, LEFT, even, odd, absorb, source, lambda x: jnp.where(x < OWN, near_row, scal[3]))


def first_right(scal, pot, coef, *refs):
    even, odd, absorb, source, later, volt, volt_1 = refs[7:]
    take_first(pot, coef, 0, END, 1, even, absorb, volt, volt_1)

    @pl.when(scal[5] == END)
    def _():
        for ref in (volt, volt_1):
            ref[END] = ref[END - 1]

    row = jnp.full((1, 128), scal[3].astype(jnp.float32))
    fields = ((volt, source), (volt_1, later))
    embed(END - 1, END, row, *fields)
    embed(END, SLOTS - 1, coef[0, ROW_AT : ROW_AT + 1], *fields)
    far_row = row_mark(coef)
    sweep(scal, RIGHT, even, odd, absorb, source, lambda x: jnp.where(x < END, scal[3], far_row))


def first_outer(scal, far, near, held, *refs):
    msg, even, odd, absorb, source, volt = refs[5:]
    take_first(far, far, POT_ROWS, 0, 1, even, absorb, volt)
    embed(1, SLAB + 1, near[0, ROW_AT : ROW_AT + 1], (volt, source))
    near_row = row_mark(near)
    sweep(scal, OUTER, even, odd, absorb, source, lambda x: jnp.where(x < OWN, near_row, scal[3]))
    for u in range(SLAB):
        msg[u] = even[OFF + OWN + u, PAD : PAD + ROWS] * (1.0 / SCALES[SWEEPS])
    msg[SLAB, 0:HEART] = held[0]
    msg[SLAB, HEART : 2 * HEART] = held[SLAB - 1]
    msg[SLAB, 2 * HEART : ROWS] = jnp.zeros((HEART, 128), jnp.float32)


def second_open(scal, own, on, held, first, even, odd, volt, out, copy):
    def keep(u, carry):
        copy[u, 0:ROWS] = own[u]
        copy[u, ROWS : ROWS + HEART] = first[u, V1_AT : V1_AT + HEART]
        put_heart(volt, u + 1, held[u])
        return carry

    lax.fori_loop(0, SLAB, keep, 0)
    clear_edges(even, odd)
    take(own, OWN, 1, even)
    take(on, END - 1, -1, even)
    put_heart(volt, SLAB + 1, on[SLAB, HEART : 2 * HEART])
    settle(1, SLAB, scal[3], even, volt, out)


def second_inner(scal, absorb, source, *refs):
    even, odd = refs[2:]
    sweep(scal, INNER, even, odd, absorb, source, lambda x: scal[3])


def second_left(scal, near, mark, absorb, source, *refs):
    even, odd, volt, out = refs[4:]
    take(near, OWN - 1, -1, even)
    put_heart(volt, 0, near[SLAB, 0:HEART])

    @pl.when(scal[4] == OWN)
    def _():
        volt[0] = volt[1]

    settle(0, 1, scal[3], even, volt, out)
    near_row = row_mark(mark)
    sweep(scal, LEFT, even, odd, absorb, source, lambda x: jnp.where(x < OWN, near_row, scal[3]))


def second_right(scal, on2, mark, absorb, source, *refs):
    even, odd = refs[2:]
    take(on2, END, 1, even)
    far_row = row_mark(mark)
    sweep(scal, RIGHT, even, odd, absorb, source, lambda x: jnp.where(x < END, scal[3], far_row))


def second_outer(scal, far, near, absorb, voltage, *refs):
    outs, (even, odd, source, volt_1), (joined,) = refs[4:8], refs[8:12], refs[12:]
    take(far, 0, 1, even)

    def plane(u, carry):
        put_heart(volt_1, u, far[u, ROWS : ROWS + HEART])
        return carry

    lax.fori_loop(0, SLAB, plane, 0)
    embed(1, SLAB + 1, near[0, ROW_AT : ROW_AT + 1], (volt_1, source))
    near_row = row_mark(near)
    sweep(scal, OUTER, even, odd, absorb, source, lambda x: jnp.where(x < OWN, near_row, scal[3]))
    sec, flip = scal[0], scal[2]

    def give(u, carry):
        joined[u, 0:ROWS] = even[OFF + OWN + u, PAD : PAD + ROWS] * (1.0 / SCALES[SWEEPS])
        joined[u, ROWS : ROWS + HEART] = voltage[u]
        x = jnp.where(flip == 1, SLAB - 1 - u, u)
        for number in range(4):
            at = pl.multiple_of((sec ^ number) * HEART, HEART)
            outs[number][x] = joined[u, pl.ds(at, HEART)]
        return carry

    lax.fori_loop(0, SLAB, give, 0)


def spread_kernel(scal, own, got_1, got_2, got_3, out, done):
    copies = []
    for number, ref in enumerate((own, got_1, got_2, got_3)):
        at = pl.ds(pl.multiple_of(scal[6 + number] * SLAB, SLAB), SLAB)
        copies.append(pltpu.make_async_copy(ref, out.at[at], done.at[number]))
    for copy in copies:
        copy.start()
    for copy in copies:
        copy.wait()


def chain(sections, bricks):
    order = []
    for brick in range(bricks):
        forward = (brick + brick // 4) % 2 == 1
        for step in range(sections):
            sec = step if forward else sections - 1 - step
            order.append(sec * bricks + brick)
    return order


VMEM = pl.BlockSpec(memory_space=pltpu.VMEM)
SMEM = pl.BlockSpec(memory_space=pltpu.SMEM)


def call(kernel, args, outs, planes, scratch=(), state=(), limit=20):
    arrays = [jax.ShapeDtypeStruct(shape, jnp.float32) for shape in outs]
    arrays += [jax.ShapeDtypeStruct(ref.shape, ref.dtype) for ref in state]
    return pl.pallas_call(
        kernel,
        out_shape=arrays,
        in_specs=[SMEM] + [VMEM] * (len(args) + len(state) - 1),
        out_specs=[VMEM] * len(arrays),
        scratch_shapes=[pltpu.VMEM(shape, jnp.float32) for shape in scratch],
        input_output_aliases={len(args) + n: len(outs) + n for n in range(len(state))},
        compiler_params=pltpu.CompilerParams(vmem_limit_bytes=limit << 20),
        cost_estimate=pl.CostEstimate(
            flops=planes * 200_000, bytes_accessed=planes * 100_000, transcendentals=0
        ),
    )(*args, *state)


def body(potentials, coefficient, recovery, excitable, row_of):
    pot, coef = potentials[0], coefficient[0]
    sections, bricks = lax.axis_size("sec"), lax.axis_size("brick")
    order = chain(sections, bricks)
    count = len(order)
    last = count - 1
    partner = [(order[i], order[i ^ 1]) for i in range(count)]
    facing = []
    for i in range(1, last, 2):
        facing += [(order[i], order[i + 1]), (order[i + 1], order[i])]
    beyond = [(order[i], order[i + 2]) for i in range(0, count - 2, 2)]
    beyond += [(order[i], order[i - 2]) for i in range(3, count, 2)]

    def across(number):
        return [(sec, sec ^ number) for sec in range(sections)]

    sec = lax.axis_index("sec")
    brick = lax.axis_index("brick")
    forward = (brick + brick // 4) % 2 == 1

    def chunk_of(section):
        return jnp.where(forward, section, sections - 1 - section)

    chunk = chunk_of(sec)
    place = brick * sections + chunk
    no_facing = (place == 0) | (place == last)
    partner_end = (place == 1) | (place == last - 1)
    scal = jnp.stack(
        [
            sec,
            chunk,
            chunk % 2,
            row_of[0],
            jnp.where(no_facing, OWN, 0),
            jnp.where(partner_end, OWN + 2 * SLAB, SLOTS),
        ]
        + [chunk_of(sec ^ number) for number in range(4)]
    ).astype(jnp.int32)

    def swapped(value):
        got = [lax.dynamic_slice_in_dim(value, SLAB * chunk, SLAB, 0)]
        for number in (1, 2, 3):
            piece = lax.dynamic_slice_in_dim(value, SLAB * chunk_of(sec ^ number), SLAB, 0)
            got.append(lax.ppermute(piece, "sec", across(number)))
        return got

    got_pot = swapped(pot)
    got_coef = swapped(coef)
    (msg_pot,) = call(gather_pot, (scal, *got_pot), [(SLAB, POT_ROWS, 128)], 10)
    msg_coef, aux = call(
        gather_coef,
        (scal, recovery, excitable, msg_pot, *got_coef),
        [(SLAB, COEF_ROWS, 128), (3, SLAB, HEART, 128)],
        20,
        scratch=[(SLAB, 128, 128)],
    )

    phi = (SLOTS + 2, PHI_PAD, 128)
    wide = (SLOTS, ROWS, 128)
    volt = (SLOTS, V_PAD, 128)
    heart = (SLAB, HEART, 128)

    def move(value, pairs):
        return lax.ppermute(value, AXES, pairs)

    near_pot = move(msg_pot, facing)
    near_coef = move(msg_coef, facing)
    on_pot = move(msg_pot, partner)
    on_coef = move(msg_coef, partner)
    (copy,) = call(first_open, (scal, msg_pot, msg_coef), [(SLAB, FAR_ROWS, 128)], 5)
    far = move(copy, beyond)
    state = call(
        first_inner,
        (scal, msg_pot, msg_coef, on_pot, on_coef, aux),
        [phi, phi, wide, wide, wide, volt, volt, heart],
        56,
    )
    on2_pot = move(near_pot, partner)
    on2_coef = move(near_coef, partner)
    *state, held = call(first_left, (scal, near_pot, near_coef, aux), [], 64, state=state)
    even, odd, absorb, source, later, volt_0, volt_1 = call(
        first_right, (scal, on2_pot, on2_coef), [], 64, state=state
    )
    message, _, _, absorb, _, _ = call(
        first_outer,
        (scal, far, near_coef, held),
        [(SLAB + 1, ROWS, 128)],
        184,
        state=[even, odd, absorb, source, volt_0],
    )

    near = move(message, facing)
    on = move(message, partner)
    even, odd, volt_2, voltage, copy = call(
        second_open,
        (scal, message, on, held, msg_coef),
        [phi, phi, (SLAB + 2, V_PAD, 128), heart, (SLAB, ROWS + HEART, 128)],
        20,
    )
    far = move(copy, beyond)
    even, odd = call(second_inner, (scal, absorb, later), [], 56, state=[even, odd])
    on2 = move(near, partner)
    even, odd, _, voltage = call(
        second_left,
        (scal, near, near_coef, absorb, later),
        [],
        64,
        state=[even, odd, volt_2, voltage],
    )
    even, odd = call(second_right, (scal, on2, on2_coef, absorb, later), [], 64, state=[even, odd])
    outs = call(
        second_outer,
        (scal, far, near_coef, absorb, voltage),
        [heart] * 4,
        184,
        scratch=[(SLAB, 128, 128)],
        state=[even, odd, later, volt_1],
    )[:4]
    back = [outs[0]]
    for number in (1, 2, 3):
        back.append(lax.ppermute(outs[number], "sec", across(number)))
    result = pl.pallas_call(
        spread_kernel,
        out_shape=jax.ShapeDtypeStruct((sections * SLAB, HEART, 128), jnp.float32),
        in_specs=[SMEM] + [VMEM] * 4,
        out_specs=pl.BlockSpec(memory_space=pl.ANY),
        scratch_shapes=[pltpu.SemaphoreType.DMA((4,))],
        compiler_params=pltpu.CompilerParams(vmem_limit_bytes=20 << 20),
        name="spread",
    )(scal, *back)
    return result[None]


def solution(mesh):
    in_specs = (
        P("sec", "brick", None, None),
        P("sec", "brick", None, None),
        P("brick", None, None),
        P("brick", None, None),
        P("brick"),
    )
    out_specs = P("sec", "brick", None, None)
    return jax.shard_map(body, mesh=mesh, in_specs=in_specs, out_specs=out_specs, check_vma=False)
```

```python
import jax
import jax.numpy as jnp
from jax import lax
from jax.experimental import pallas as pl
from jax.experimental.pallas import tpu as pltpu
from jax.sharding import PartitionSpec as P

SUBSTEPS = 8
SWEEPS = 16

coupling_gain = 0.1
ionic_timestep = 0.05
ionic_gain = 8.0
recovery_rate = 0.1
recovery_decay = 0.5
spectrum_low = 0.04
spectrum_high = 12.32

SLAB = 8
ROWS = 96
HEART = 32
SLOTS = 40
OWN = 16
OFF = 1
PAD = 8
PART = 16
PARTS = ROWS // PART
AXES = ("sec", "brick")
V0_AT, POT_ROWS = 96, 128
V1_AT, ROW_AT, COEF_ROWS = 96, 128, 136
FAR_ROWS = POT_ROWS + ROWS
PHI_PAD = 112
V_PAD = 48


def chebyshev_weights(count):
    center = 0.5 * (spectrum_high + spectrum_low)
    spread = 0.5 * (spectrum_high - spectrum_low)
    ratio = center / spread
    current = 1.0 / ratio
    weights = [(0.0, 1.0 / center)]
    for _ in range(count):
        following = 1.0 / (2.0 * ratio - current)
        weights.append((following * current, 2.0 * following / spread))
        current = following
    return weights


WEIGHTS = chebyshev_weights(SWEEPS - 1)
SHIFT = 6.0 - 0.5 * (spectrum_high + spectrum_low)


def ionic(voltage, recovery, threshold, active):
    for _ in range(SUBSTEPS):
        drive = ionic_gain * voltage * (voltage - threshold) * (1.0 - voltage) - recovery
        relax = recovery_rate * (voltage - recovery_decay * recovery)
        voltage = voltage + ionic_timestep * active * drive
        recovery = recovery + ionic_timestep * active * relax
    return voltage, recovery


def lanes(shape):
    return lax.broadcasted_iota(jnp.int32, shape, len(shape) - 1)


def side_sum_zero(value):
    lane = lanes(value.shape)
    before = jnp.where(lane == 0, 0.0, pltpu.roll(value, 1, 1))
    after = jnp.where(lane == 127, 0.0, pltpu.roll(value, 127, 1))
    return before + after


def side_sum_edge(value):
    lane = lanes(value.shape)
    before = jnp.where(lane == 0, value, pltpu.roll(value, 1, 1))
    after = jnp.where(lane == 127, value, pltpu.roll(value, 127, 1))
    return before + after


def heart_laplace(ref, x):
    here = ref[x, PAD : PAD + HEART]
    total = ref[x - 1, PAD : PAD + HEART] + ref[x + 1, PAD : PAD + HEART]
    total = total + ref[x, PAD - 1 : PAD - 1 + HEART] + ref[x, PAD + 1 : PAD + 1 + HEART]
    return total + side_sum_edge(here) - 6.0 * here


def put_heart(ref, x, value):
    ref[x, PAD : PAD + HEART] = value
    ref[x, PAD - 1 : PAD] = value[0:1]
    ref[x, PAD + HEART : PAD + HEART + 1] = value[HEART - 1 : HEART]


def torso_current(ref, x, row):
    at = PAD + HEART * row
    here = ref[x, at : at + HEART]
    total = ref[x - 1, at : at + HEART] + ref[x + 1, at : at + HEART]
    total = total + ref[x, at - 1 : at - 1 + HEART] + ref[x, at + 1 : at + 1 + HEART]
    return total + side_sum_zero(here) - 6.0 * here


def halves(value):
    high = value.astype(jnp.bfloat16)
    return high, (value - high.astype(jnp.float32)).astype(jnp.bfloat16)


def sweep(scal, plan, even, odd, absorb, source):
    accs = [pltpu.ACC(part % 2)((PART, 256), jnp.float32) for part in range(2 * PARTS)]
    pl.run_scoped(lambda *refs: sweep_with(scal, plan, even, odd, absorb, source, refs), *accs)


def sweep_with(scal, plan, even, odd, absorb, source, accs):
    accs = (accs[:PARTS], accs[PARTS:])
    low_end, high_end = scal[4], scal[5]
    row = lax.broadcasted_iota(jnp.int32, (256, 256), 0)
    column = lax.broadcasted_iota(jnp.int32, (256, 256), 1)
    same = (row >= 128) == (column >= 128)
    apart = jnp.abs(row - column)
    beside = ((same & (apart == 1)) | (apart == 128)).astype(jnp.bfloat16)
    none = jnp.zeros((PART, 256), jnp.bfloat16)
    for unit in range(2):
        pltpu.matmul_push_rhs(beside, 0, unit)
    for number, acc in enumerate(accs[0] + accs[1]):
        pltpu.matmul_acc_lhs(acc, none, load_staged_rhs=0 if number < 2 else None)
    for acc in accs[0] + accs[1]:
        pltpu.matmul_pop(acc)

    def place(number, pair):
        _, runs = plan[number]
        first, size = runs[0]
        x = first + 2 * pair
        if len(runs) == 1:
            return x
        skip = runs[1][0] - first - size
        if isinstance(pair, int):
            return x + (skip if 2 * pair >= size else 0)
        return x + jnp.where(2 * pair >= size, skip, 0)

    def begin(number, pair, acc):
        level = plan[number][0]
        src = even if level % 2 else odd
        x = place(number, pair) + OFF
        for part in range(PARTS):
            at, to = PAD + PART * part, PAD + PART * (part + 1)
            high_0, low_0 = halves(src[x, at:to])
            high_1, low_1 = halves(src[x + 1, at:to])
            pltpu.matmul_acc_lhs(acc[part], jnp.concatenate([high_0, high_1], 1))
            pltpu.matmul_acc_lhs(acc[part], jnp.concatenate([low_0, low_1], 1))

    def finish(number, pair, acc):
        level = plan[number][0]
        src, dst = (even, odd) if level % 2 else (odd, even)
        x = place(number, pair)
        keeps, pushes = [], []
        for plane in range(2):
            inside = (x + plane >= low_end) & (x + plane < high_end)
            keeps.append(jnp.where(inside, WEIGHTS[level - 1][0], 0.0).astype(jnp.float32))
            pushes.append(jnp.where(inside, WEIGHTS[level - 1][1], 0.0).astype(jnp.float32))
        for part in range(PARTS):
            start, stop = PART * part, PART * (part + 1)
            at, to = PAD + start, PAD + stop
            sums = pltpu.matmul_pop(acc[part])
            for plane in range(2):
                here = x + plane
                total = src[here + OFF - 1 + 2 * plane, at:to]
                total = total + (src[here + OFF, at - 1 : to - 1] + src[here + OFF, at + 1 : to + 1])
                total = total + source[here, start:stop]
                total = total - absorb[here, start:stop] * src[here + OFF, at:to]
                total = pushes[plane] * (total + sums[:, 128 * plane : 128 * (plane + 1)])
                if level > 1:
                    total = total - keeps[plane] * dst[here + OFF, at:to]
                dst[here + OFF, at:to] = total

    one, other = accs
    begin(0, 0, one)
    for number, (_, runs) in enumerate(plan):
        pairs = sum(size for _, size in runs) // 2
        steps = (pairs - 1) // 2

        def two_pairs(step, carry, number=number, one=one, other=other):
            begin(number, 2 * step + 1, other)
            finish(number, 2 * step, one)
            begin(number, 2 * step + 2, one)
            finish(number, 2 * step + 1, other)
            return carry

        if steps:
            lax.fori_loop(0, steps, two_pairs, 0)
        pair = 2 * steps
        if pairs - pair == 2:
            begin(number, pair + 1, other)
            finish(number, pair, one)
            pair, one, other = pair + 1, other, one
        following = number + 1 < len(plan)
        if following and pairs > 2:
            begin(number + 1, 0, other)
        finish(number, pair, one)
        if following and pairs <= 2:
            begin(number + 1, 0, other)
        one, other = other, one


END = OWN + 2 * SLAB
INNER = [(k, [(OWN + k, 2 * SLAB - 2 * k)]) for k in range(1, SLAB)]
LEFT = [(k, [(SLAB + k, SLAB)]) for k in range(1, SLAB + 1)]
RIGHT = [(k, [(END - k, SLAB)]) for k in range(1, SLAB + 1)]
OUTER = [(k, [(k, SLAB)]) for k in range(1, SLAB + 1)]
OUTER += [(k, [(k, SLOTS - 2 * k)]) for k in range(SLAB + 1, SWEEPS + 1)]


def clear_edges(even, odd):
    zero = jnp.zeros((PAD, 128), jnp.float32)

    def edge(x, carry):
        for ref in (even, odd):
            ref[x, 0:PAD] = zero
            ref[x, PAD + ROWS : PHI_PAD] = zero
        return carry

    lax.fori_loop(0, SLOTS + 2, edge, 0)


def collect(scal, own, got, u, out):
    sec, chunk, flip = scal[0], scal[1], scal[2]
    x = jnp.where(flip == 1, SLAB - 1 - u, u)
    for number, ref in enumerate((own, *got)):
        at = pl.multiple_of((sec ^ number) * HEART, HEART)
        out[u, pl.ds(at, HEART)] = ref[x]
    return SLAB * chunk + x


def gather_pot(scal, own, got_1, got_2, got_3, msg):
    def plane(u, carry):
        collect(scal, own, (got_1, got_2, got_3), u, msg)
        return carry

    lax.fori_loop(0, SLAB, plane, 0)


def gather_coef(scal, rec, exc, pot, own, got_1, got_2, got_3, msg, far, aux, deep):
    strip = jnp.full((8, 128), scal[3].astype(jnp.float32))

    def plane(u, carry):
        whole = collect(scal, own, (got_1, got_2, got_3), u, deep)
        msg[u, 0:ROWS] = deep[u, 0:ROWS]
        far[u, 0:POT_ROWS] = pot[u]
        far[u, POT_ROWS:FAR_ROWS] = deep[u, 0:ROWS]
        threshold = deep[u, ROWS : ROWS + HEART]
        active = exc[whole].astype(jnp.float32)
        voltage, recovery = ionic(pot[u, V0_AT : V0_AT + HEART], rec[whole], threshold, active)
        msg[u, V1_AT : V1_AT + HEART] = voltage
        msg[u, ROW_AT : ROW_AT + 8] = strip
        aux[0, u] = threshold
        aux[1, u] = recovery
        aux[2, u] = active
        return carry

    lax.fori_loop(0, SLAB, plane, 0)


def take(ref, first, step, even):
    def plane(u, carry):
        even[first + step * u + OFF, PAD : PAD + ROWS] = ref[u, 0:ROWS]
        return carry

    lax.fori_loop(0, SLAB, plane, 0)


def take_first(pot, coef, at, first, step, even, absorb, volt, volt_1=None):
    def plane(u, carry):
        x = first + step * u
        even[x + OFF, PAD : PAD + ROWS] = pot[u, 0:ROWS]
        absorb[x] = coef[u, at : at + ROWS] + SHIFT
        put_heart(volt, x, pot[u, V0_AT : V0_AT + HEART])
        if volt_1 is not None:
            put_heart(volt_1, x, coef[u, V1_AT : V1_AT + HEART])
        return carry

    lax.fori_loop(0, SLAB, plane, 0)


def embed(low, high, mark, *fields):
    mark = jnp.broadcast_to(mark, (HEART, 128))

    def plane(x, carry):
        for ref, out in fields:
            gain = heart_laplace(ref, x)
            for layer in range(3):
                out[x, layer * HEART : (layer + 1) * HEART] = jnp.where(mark == layer, gain, 0.0)
        return carry

    lax.fori_loop(low, high, plane, 0)


def on_layer(row, work):
    for layer in range(3):

        @pl.when(row == layer)
        def _():
            work(layer)


def couple(first, last, row, even, volt_1, aux, held):
    def work(layer):
        def plane(u, carry):
            x = OWN + u
            gain = heart_laplace(volt_1, x) + torso_current(even, x + OFF, layer)
            voltage = volt_1[x, PAD : PAD + HEART] + coupling_gain * gain
            held[u], _ = ionic(voltage, aux[1, u], aux[0, u], aux[2, u])
            return carry

        lax.fori_loop(first, last, plane, 0)

    on_layer(row, work)


def settle(first, last, row, even, volt, out):
    def work(layer):
        def plane(u, carry):
            gain = heart_laplace(volt, u + 1) + torso_current(even, OWN + OFF + u, layer)
            out[u] = volt[u + 1, PAD : PAD + HEART] + coupling_gain * gain
            return carry

        lax.fori_loop(first, last, plane, 0)

    on_layer(row, work)


def first_inner(scal, pot, coef, on_pot, on_coef, aux, *refs):
    even, odd, absorb, source, later, volt, volt_1, held = refs
    clear_edges(even, odd)
    take_first(pot, coef, 0, OWN, 1, even, absorb, volt, volt_1)
    take_first(on_pot, on_coef, 0, END - 1, -1, even, absorb, volt, volt_1)
    row = jnp.full((1, 128), scal[3].astype(jnp.float32))
    embed(OWN + 1, END - 1, row, (volt, source), (volt_1, later))
    couple(1, SLAB, scal[3], even, volt_1, aux, held)
    sweep(scal, INNER, even, odd, absorb, source)


def first_left(scal, pot, coef, aux, *refs):
    even, odd, absorb, source, later, volt, volt_1, held = refs[8:]
    take_first(pot, coef, 0, OWN - 1, -1, even, absorb, volt, volt_1)

    @pl.when(scal[4] == OWN)
    def _():
        for ref in (volt, volt_1):
            ref[OWN - 1] = ref[OWN]

    row = jnp.full((1, 128), scal[3].astype(jnp.float32))
    fields = ((volt, source), (volt_1, later))
    embed(SLAB + 1, OWN, coef[0, ROW_AT : ROW_AT + 1], *fields)
    embed(OWN, OWN + 1, row, *fields)
    couple(0, 1, scal[3], even, volt_1, aux, held)
    sweep(scal, LEFT, even, odd, absorb, source)


def first_right(scal, pot, coef, *refs):
    even, odd, absorb, source, later, volt, volt_1 = refs[7:]
    take_first(pot, coef, 0, END, 1, even, absorb, volt, volt_1)

    @pl.when(scal[5] == END)
    def _():
        for ref in (volt, volt_1):
            ref[END] = ref[END - 1]

    row = jnp.full((1, 128), scal[3].astype(jnp.float32))
    fields = ((volt, source), (volt_1, later))
    embed(END - 1, END, row, *fields)
    embed(END, SLOTS - 1, coef[0, ROW_AT : ROW_AT + 1], *fields)
    sweep(scal, RIGHT, even, odd, absorb, source)


def first_outer(scal, far, near, held, first, *refs):
    msg, copy, even, odd, absorb, source, volt = refs[5:]
    take_first(far, far, POT_ROWS, 0, 1, even, absorb, volt)
    embed(1, SLAB + 1, near[0, ROW_AT : ROW_AT + 1], (volt, source))
    sweep(scal, OUTER, even, odd, absorb, source)
    for u in range(SLAB):
        msg[u] = even[OFF + OWN + u, PAD : PAD + ROWS]
        copy[u, 0:ROWS] = even[OFF + OWN + u, PAD : PAD + ROWS]
        copy[u, ROWS : ROWS + HEART] = first[u, V1_AT : V1_AT + HEART]
    msg[SLAB, 0:HEART] = held[0]
    msg[SLAB, HEART : 2 * HEART] = held[SLAB - 1]
    msg[SLAB, 2 * HEART : ROWS] = jnp.zeros((HEART, 128), jnp.float32)


def second_inner(scal, own, on, held, absorb, source, *refs):
    volt, out, even, odd = refs[2:]

    def keep(u, carry):
        put_heart(volt, u + 1, held[u])
        return carry

    lax.fori_loop(0, SLAB, keep, 0)
    take(own, OWN, 1, even)
    take(on, END - 1, -1, even)
    put_heart(volt, SLAB + 1, on[SLAB, HEART : 2 * HEART])
    settle(1, SLAB, scal[3], even, volt, out)
    sweep(scal, INNER, even, odd, absorb, source)


def second_left(scal, near, absorb, source, *refs):
    even, odd, volt, out = refs[4:]
    take(near, OWN - 1, -1, even)
    put_heart(volt, 0, near[SLAB, 0:HEART])

    @pl.when(scal[4] == OWN)
    def _():
        volt[0] = volt[1]

    settle(0, 1, scal[3], even, volt, out)
    sweep(scal, LEFT, even, odd, absorb, source)


def second_right(scal, on2, absorb, source, *refs):
    even, odd = refs[2:]
    take(on2, END, 1, even)
    sweep(scal, RIGHT, even, odd, absorb, source)


def second_outer(scal, far, near, absorb, voltage, *refs):
    outs, (even, odd, source, volt_1), (joined,) = refs[4:8], refs[8:12], refs[12:]
    take(far, 0, 1, even)

    def plane(u, carry):
        put_heart(volt_1, u, far[u, ROWS : ROWS + HEART])
        return carry

    lax.fori_loop(0, SLAB, plane, 0)
    embed(1, SLAB + 1, near[0, ROW_AT : ROW_AT + 1], (volt_1, source))
    sweep(scal, OUTER, even, odd, absorb, source)
    sec, flip = scal[0], scal[2]

    def give(u, carry):
        joined[u, 0:ROWS] = even[OFF + OWN + u, PAD : PAD + ROWS]
        joined[u, ROWS : ROWS + HEART] = voltage[u]
        x = jnp.where(flip == 1, SLAB - 1 - u, u)
        for number in range(4):
            at = pl.multiple_of((sec ^ number) * HEART, HEART)
            outs[number][x] = joined[u, pl.ds(at, HEART)]
        return carry

    lax.fori_loop(0, SLAB, give, 0)


def spread_kernel(scal, own, got_1, got_2, got_3, out):
    for number, ref in enumerate((own, got_1, got_2, got_3)):
        at = scal[6 + number] * SLAB
        for u in range(SLAB):
            out[at + u] = ref[u]


def chain(sections, bricks):
    order = []
    for brick in range(bricks):
        forward = (brick + brick // 4) % 2 == 1
        for step in range(sections):
            sec = step if forward else sections - 1 - step
            order.append(sec * bricks + brick)
    return order


VMEM = pl.BlockSpec(memory_space=pltpu.VMEM)
SMEM = pl.BlockSpec(memory_space=pltpu.SMEM)


def call(kernel, args, outs, planes, scratch=(), state=(), limit=20):
    arrays = [jax.ShapeDtypeStruct(shape, jnp.float32) for shape in outs]
    arrays += [jax.ShapeDtypeStruct(ref.shape, ref.dtype) for ref in state]
    return pl.pallas_call(
        kernel,
        out_shape=arrays,
        in_specs=[SMEM] + [VMEM] * (len(args) + len(state) - 1),
        out_specs=[VMEM] * len(arrays),
        scratch_shapes=[pltpu.VMEM(shape, jnp.float32) for shape in scratch],
        input_output_aliases={len(args) + n: len(outs) + n for n in range(len(state))},
        compiler_params=pltpu.CompilerParams(vmem_limit_bytes=limit << 20),
        cost_estimate=pl.CostEstimate(
            flops=planes * 200_000, bytes_accessed=planes * 100_000, transcendentals=0
        ),
    )(*args, *state)


def body(potentials, coefficient, recovery, excitable, row_of):
    pot, coef = potentials[0], coefficient[0]
    sections, bricks = lax.axis_size("sec"), lax.axis_size("brick")
    order = chain(sections, bricks)
    count = len(order)
    last = count - 1
    partner = [(order[i], order[i ^ 1]) for i in range(count)]
    facing = []
    for i in range(1, last, 2):
        facing += [(order[i], order[i + 1]), (order[i + 1], order[i])]
    beyond = [(order[i], order[i + 2]) for i in range(0, count - 2, 2)]
    beyond += [(order[i], order[i - 2]) for i in range(3, count, 2)]

    def across(number):
        return [(sec, sec ^ number) for sec in range(sections)]

    sec = lax.axis_index("sec")
    brick = lax.axis_index("brick")
    forward = (brick + brick // 4) % 2 == 1

    def chunk_of(section):
        return jnp.where(forward, section, sections - 1 - section)

    chunk = chunk_of(sec)
    place = brick * sections + chunk
    no_facing = (place == 0) | (place == last)
    partner_end = (place == 1) | (place == last - 1)
    scal = jnp.stack(
        [
            sec,
            chunk,
            chunk % 2,
            row_of[0],
            jnp.where(no_facing, OWN, 0),
            jnp.where(partner_end, OWN + 2 * SLAB, SLOTS),
        ]
        + [chunk_of(sec ^ number) for number in range(4)]
    ).astype(jnp.int32)

    def swapped(value):
        got = [lax.dynamic_slice_in_dim(value, SLAB * chunk, SLAB, 0)]
        for number in (1, 2, 3):
            piece = lax.dynamic_slice_in_dim(value, SLAB * chunk_of(sec ^ number), SLAB, 0)
            got.append(lax.ppermute(piece, "sec", across(number)))
        return got

    got_pot = swapped(pot)
    got_coef = swapped(coef)
    (msg_pot,) = call(gather_pot, (scal, *got_pot), [(SLAB, POT_ROWS, 128)], 10)
    msg_coef, copy, aux = call(
        gather_coef,
        (scal, recovery, excitable, msg_pot, *got_coef),
        [(SLAB, COEF_ROWS, 128), (SLAB, FAR_ROWS, 128), (3, SLAB, HEART, 128)],
        20,
        scratch=[(SLAB, 128, 128)],
    )

    phi = (SLOTS + 2, PHI_PAD, 128)
    wide = (SLOTS, ROWS, 128)
    volt = (SLOTS, V_PAD, 128)
    heart = (SLAB, HEART, 128)

    def move(value, pairs):
        return lax.ppermute(value, AXES, pairs)

    near_pot = move(msg_pot, facing)
    near_coef = move(msg_coef, facing)
    on_pot = move(msg_pot, partner)
    on_coef = move(msg_coef, partner)
    far = move(copy, beyond)
    state = call(
        first_inner,
        (scal, msg_pot, msg_coef, on_pot, on_coef, aux),
        [phi, phi, wide, wide, wide, volt, volt, heart],
        56,
    )
    on2_pot = move(near_pot, partner)
    on2_coef = move(near_coef, partner)
    *state, held = call(first_left, (scal, near_pot, near_coef, aux), [], 64, state=state)
    even, odd, absorb, source, later, volt_0, volt_1 = call(
        first_right, (scal, on2_pot, on2_coef), [], 64, state=state
    )
    message, copy, even, odd, absorb, _, _ = call(
        first_outer,
        (scal, far, near_coef, held, msg_coef),
        [(SLAB + 1, ROWS, 128), (SLAB, ROWS + HEART, 128)],
        184,
        state=[even, odd, absorb, source, volt_0],
    )

    near = move(message, facing)
    on = move(message, partner)
    far = move(copy, beyond)
    volt_2, voltage, even, odd = call(
        second_inner,
        (scal, message, on, held, absorb, later),
        [(SLAB + 2, V_PAD, 128), heart],
        56,
        state=[even, odd],
    )
    on2 = move(near, partner)
    even, odd, _, voltage = call(
        second_left, (scal, near, absorb, later), [], 64, state=[even, odd, volt_2, voltage]
    )
    even, odd = call(second_right, (scal, on2, absorb, later), [], 64, state=[even, odd])
    outs = call(
        second_outer,
        (scal, far, near_coef, absorb, voltage),
        [heart] * 4,
        184,
        scratch=[(SLAB, 128, 128)],
        state=[even, odd, later, volt_1],
    )[:4]
    back = [outs[0]]
    for number in (1, 2, 3):
        back.append(lax.ppermute(outs[number], "sec", across(number)))
    (result,) = call(spread_kernel, (scal, *back), [(sections * SLAB, HEART, 128)], 5)
    return result[None]


def solution(mesh):
    in_specs = (
        P("sec", "brick", None, None),
        P("sec", "brick", None, None),
        P("brick", None, None),
        P("brick", None, None),
        P("brick"),
    )
    out_specs = P("sec", "brick", None, None)
    return jax.shard_map(body, mesh=mesh, in_specs=in_specs, out_specs=out_specs, check_vma=False)
```
